32 devices in a mesh: groups: 2 (over y), row: 4 (over z), col: 4 (over x, core).
Axes of the slice: x: 2, y: 2, z: 4, core: 2. Of those that a mesh axis runs over, the one named last changes fastest.
Arguments:
- positions: float32 [2, 8, 4, 512], P(None, ('groups', 'row'), 'col'), parts along dimension 1, may hold values from 0 to 1
- genes: int32 [8, 4, 512], P(('groups', 'row'), 'col'), parts along dimension 0, may hold values from 0 to 479
- candidates: int32 [8, 4, 512, 128], P(('groups', 'row'), 'col'), parts along dimension 0, may hold values from 0 to 1151, as said below
- block_counts: int32 [8, 4, 2], P(('groups', 'row'), 'col'), parts along dimension 0, may hold values from 0 to 256, as said below
- profile_weights: float32 [480, 8, 4, 128], P(None, ('groups', 'row'), 'col'), parts along dimension 1, may hold values from 0.05 to 5
- centroids: float32 [2, 8, 4, 128], P(None, ('groups', 'row'), 'col'), parts along dimension 1, may hold values from 0 to 1
- spreads: float32 [2, 8, 4, 128], P(None, ('groups', 'row'), 'col'), parts along dimension 1, may hold values from 0.05 to 0.4
- correlation: float32 [8, 4, 128], P(('groups', 'row'), 'col'), parts along dimension 0, may hold values from -0.6 to 0.6
Outputs:
- final_profile: float32 [480, 8, 4, 128], P(None, ('groups', 'row'), 'col'), parts along dimension 1
- final_cells: float32 [6, 8, 4, 128], P(None, ('groups', 'row'), 'col'), parts along dimension 1
The draws below stay inside these ranges and needn't reach their ends.
There are 2 independent parts, one for each index of `groups`. The reference program is written for one: setup_inputs(seed, part) draws one part's arguments, and reference() takes and returns one part's arrays. A program takes and returns all parts, laid end to end along the dimension named above; each array names one. Nothing has to cross between parts.
Inputs may be any that keep to these rules, and one draw needn't show every extreme that they name: `candidates`: every candidate names a cell of the transcript's own tile or of one of the eight tiles around it that lie in the slab; an id may appear more than once in one list. `block_counts`: in each tile the blocks with a nonzero count come first, and the first block of every tile is full.
All inputs are finite; a program needn't handle non-finite values.
Results may differ from the reference program's by a relative error of at most 0.0003.
Values sent between devices are 32-bit elements; how exact they have to be, the bound alone decides.
A program may use at most 64 MiB of HBM per device.

```python
import math
import jax
import jax.numpy as jnp
import numpy as np
from jax import lax

G = 480
K = 128
CAND = 128
BLOCK = 256
NBLK = 2
ITERS = 2
TILE_ROWS = 4
TILE_COLS = 4
TOK = 512


def draw_candidates(key, part):
    key_row, key_col, key_cell = jax.random.split(key, 3)
    grid_shape = (TILE_ROWS, TILE_COLS, TOK, CAND)
    step_row = jax.random.randint(key_row, grid_shape, -1, 2)
    step_col = jax.random.randint(key_col, grid_shape, -1, 2)
    within = jax.random.randint(key_cell, grid_shape, 0, K)
    row_here = jnp.arange(TILE_ROWS, dtype=jnp.int32)[:, None, None, None]
    col_here = jnp.arange(TILE_COLS, dtype=jnp.int32)[None, :, None, None]
    home_row = jnp.clip(row_here + step_row, 0, TILE_ROWS - 1)
    home_col = jnp.clip(col_here + step_col, 0, TILE_COLS - 1)
    neighbour_slot = (home_row - row_here + 1) * 3 + (home_col - col_here + 1)
    return (neighbour_slot * K + within).astype(jnp.int32)


def draw_block_counts(key, part):
    key_live, key_filled = jax.random.split(key, 2)
    live_count = jax.random.randint(key_live, (TILE_ROWS, TILE_COLS, 1), 1, NBLK + 1)
    live_count = live_count.at[0, 0, 0].set(NBLK)
    filled = jax.random.randint(key_filled, (TILE_ROWS, TILE_COLS, NBLK), BLOCK // 4, BLOCK + 1)
    filled = filled.at[:, :, 0].set(BLOCK)
    block_ids = jnp.arange(NBLK, dtype=jnp.int32)[None, None, :]
    return jnp.where(block_ids < live_count, filled, 0).astype(jnp.int32)


def touch_ends(array, stream_key, smallest, largest):
    longest = array.shape.index(max(array.shape))
    spots = []
    for shift in (0, 1):
        where = [jax.random.randint(jax.random.fold_in(stream_key, axis), (), 0, length) for axis, length in enumerate(array.shape)]
        where[longest] = (where[longest] + shift) % array.shape[longest]
        spots.append(tuple(where))
    return array.at[spots[0]].set(smallest).at[spots[1]].set(largest)


def level_of(key, shape, shards, smallest, largest):
    level, own = 1.0, jax.random.fold_in(key, 6)
    for axis_at, blocks in shards:
        steps = jnp.exp(jax.random.uniform(jax.random.fold_in(own, axis_at), (blocks,), jnp.float32, smallest / len(shards), largest / len(shards)))
        level = level * jnp.repeat(steps, shape[axis_at] // blocks).reshape([-1 if axis == axis_at else 1 for axis in range(len(shape))])
    return level


def rank_table(amount, slope):
    loads = [(1 << 20) // math.isqrt(grade ** slope) + 1 for grade in range(1, amount + 1)]
    spread = 1 + sum(loads) // (1 << 30)
    return np.cumsum(np.array([max(1, weight // spread) for weight in loads]))


def ranked_ids(own_key, extent, amount, lean):
    table = rank_table(amount, lean)
    pick = jax.random.randint(jax.random.fold_in(own_key, 1), extent, 0, int(table[amount - 1]))
    grade = jnp.searchsorted(jnp.asarray(table, jnp.int32), pick, side="right")
    return jax.random.permutation(jax.random.fold_in(own_key, 2), amount)[grade].astype(jnp.int32)


def setup_inputs(seed: int = 0, part: int = 0) -> dict:
    key_of = jax.random.split(jax.random.key(seed), 9)
    own_keys = jax.random.split(jax.random.fold_in(key_of[8], part), 9)
    return {
        "positions": jnp.clip(1.0 * jax.random.uniform(own_keys[0], (2, TILE_ROWS, TILE_COLS, TOK), jnp.float32) ** level_of(own_keys[0], (2, TILE_ROWS, TILE_COLS, TOK), ((1, 4), (2, 4)), -0.2, 0.2), 0.0, 1.0),
        "genes": touch_ends(ranked_ids(own_keys[1], (TILE_ROWS, TILE_COLS, TOK), G, 2), jax.random.fold_in(own_keys[1], 3), 0, G - 1).astype(jnp.int32),
        "candidates": draw_candidates(jax.random.fold_in(jax.random.fold_in(key_of[8], part), 71), part),
        "block_counts": draw_block_counts(jax.random.fold_in(jax.random.fold_in(key_of[8], part), 71), part),
        "profile_weights": jnp.clip(jnp.exp(math.log(5.0) - 4.6051702 * jax.random.uniform(own_keys[4], (G, TILE_ROWS, TILE_COLS, K), jnp.float32) ** level_of(own_keys[4], (G, TILE_ROWS, TILE_COLS, K), ((1, 4), (2, 4)), -0.2, 0.2)), 0.05, 5.0),
        "centroids": jnp.clip(1.0 * jax.random.uniform(own_keys[5], (2, TILE_ROWS, TILE_COLS, K), jnp.float32) ** level_of(own_keys[5], (2, TILE_ROWS, TILE_COLS, K), ((1, 4), (2, 4)), -0.2, 0.2), 0.0, 1.0),
        "spreads": jnp.clip(jnp.exp(math.log(0.4) - 2.0794415 * jax.random.uniform(own_keys[6], (2, TILE_ROWS, TILE_COLS, K), jnp.float32) ** level_of(own_keys[6], (2, TILE_ROWS, TILE_COLS, K), ((1, 4), (2, 4)), -0.2, 0.2)), 0.05, 0.4),
        "correlation": jnp.clip(jax.random.uniform(own_keys[7], (TILE_ROWS, TILE_COLS, K), jnp.float32, -0.6, 0.6) * level_of(own_keys[7], (TILE_ROWS, TILE_COLS, K), ((0, 4), (1, 4)), -0.4, 0.0), -0.6, 0.6),
    }


pseudo_count = 0.05
prior_weight = 1.0

def cell_terms(profile, cov_rr, cov_rc, cov_cc, log_weight):
    determinant = cov_rr * cov_cc - cov_rc * cov_rc
    return (jnp.log(profile), cov_cc / determinant, -cov_rc / determinant, cov_rr / determinant, log_weight - 0.5 * jnp.log(determinant))

def update_cells(gene_counts, moments, centre_row, centre_col, cov_rr, cov_rc, cov_cc):
    weight_sum, sum_row, sum_col, sum_rr, sum_rc, sum_cc = moments
    gene_total = gene_counts.shape[0]
    profile = (gene_counts + pseudo_count) / (lax.optimization_barrier(jnp.sum(gene_counts, axis=0)) + gene_total * pseudo_count)
    new_row = (sum_row + prior_weight * centre_row) / (weight_sum + prior_weight)
    new_col = (sum_col + prior_weight * centre_col) / (weight_sum + prior_weight)
    scatter_rr = sum_rr - 2.0 * new_row * sum_row + weight_sum * new_row * new_row
    scatter_rc = sum_rc - new_row * sum_col - new_col * sum_row + weight_sum * new_row * new_col
    scatter_cc = sum_cc - 2.0 * new_col * sum_col + weight_sum * new_col * new_col
    denominator = weight_sum + prior_weight
    return (profile, new_row, new_col, (scatter_rr + prior_weight * cov_rr) / denominator, (scatter_rc + prior_weight * cov_rc) / denominator, (scatter_cc + prior_weight * cov_cc) / denominator, jnp.log(weight_sum + 1.0))

def cell_summary(centre_row, centre_col, cov_rr, cov_rc, cov_cc, log_weight):
    return jnp.stack([centre_row, centre_col, 0.5 * jnp.log(cov_rr), 0.5 * jnp.log(cov_cc), cov_rc / jnp.sqrt(cov_rr * cov_cc), log_weight])

def reference(positions, genes, candidates, block_counts, profile_weights, centroids, spreads, correlation):
    gene_total, tile_rows, tile_cols, tile_cells = profile_weights.shape
    cell_count = tile_rows * tile_cols * tile_cells
    tile_tokens = genes.shape[2]
    profile = (profile_weights / lax.optimization_barrier(jnp.sum(profile_weights, axis=0, keepdims=True))).reshape(gene_total, cell_count)
    centre_row = centroids[0].reshape(cell_count)
    centre_col = centroids[1].reshape(cell_count)
    spread_row = spreads[0].reshape(cell_count)
    spread_col = spreads[1].reshape(cell_count)
    cov_rr = spread_row * spread_row
    cov_cc = spread_col * spread_col
    cov_rc = correlation.reshape(cell_count) * spread_row * spread_col
    log_weight = jnp.zeros((cell_count,), jnp.float32)
    tile_of_cell = jnp.arange(cell_count, dtype=jnp.int32) // tile_cells
    home_row = tile_of_cell // tile_cols
    home_col = tile_of_cell % tile_cols
    token_ids = jnp.arange(tile_tokens, dtype=jnp.int32)
    valid_rows = ((token_ids % BLOCK)[None, None, :] < block_counts[:, :, token_ids // BLOCK]).astype(jnp.float32)
    column_ids = jnp.arange(tile_cols, dtype=jnp.int32)[:, None, None]
    slot_ids = jnp.arange(CAND, dtype=jnp.int32)
    earlier = slot_ids[None, :] < slot_ids[:, None]
    for iteration in range(ITERS):
        log_table, prec_rr, prec_rc, prec_cc, cell_bias = cell_terms(profile, cov_rr, cov_rc, cov_cc, log_weight)

        def tile_row(accum, row_index):
            count_acc, moment_acc = accum
            local_ids = candidates[row_index]
            neighbour_slot = local_ids // tile_cells
            cand_row = row_index + neighbour_slot // 3 - 1
            cand_col = column_ids + neighbour_slot % 3 - 1
            candidate_ids = ((cand_row * tile_cols + cand_col) * tile_cells + local_ids % tile_cells).astype(jnp.int32)
            pos_row = positions[0, row_index][..., None]
            pos_col = positions[1, row_index][..., None]
            gene_row = genes[row_index][..., None]
            shift_row = (home_row[candidate_ids] - row_index).astype(jnp.float32)
            shift_col = (home_col[candidate_ids] - column_ids).astype(jnp.float32)
            delta_row = pos_row - (centre_row[candidate_ids] + shift_row)
            delta_col = pos_col - (centre_col[candidate_ids] + shift_col)
            score = log_table[gene_row, candidate_ids] + cell_bias[candidate_ids] - 0.5 * (prec_rr[candidate_ids] * delta_row * delta_row + 2.0 * prec_rc[candidate_ids] * delta_row * delta_col + prec_cc[candidate_ids] * delta_col * delta_col)
            row_max = lax.optimization_barrier(jnp.max(score, axis=-1, keepdims=True))
            exp_terms = jnp.exp(score - row_max)
            posterior = exp_terms / lax.optimization_barrier(jnp.sum(exp_terms, axis=-1, keepdims=True)) * valid_rows[row_index][..., None]
            same_cell = candidate_ids[..., :, None] == candidate_ids[..., None, :]
            joint_share = lax.optimization_barrier(jnp.sum(jnp.where(same_cell, posterior[..., None, :], 0.0), axis=-1))
            repeat = jnp.any(same_cell & earlier, axis=-1)
            rounded_share = lax.optimization_barrier(joint_share.astype(jnp.bfloat16)).astype(jnp.float32)
            rounded_share = jnp.where(repeat, 0.0, rounded_share)
            count_acc = count_acc.at[gene_row, candidate_ids].add(rounded_share)
            local_row = pos_row - shift_row
            local_col = pos_col - shift_col
            moment_terms = jnp.stack([posterior, posterior * local_row, posterior * local_col, posterior * local_row * local_row, posterior * local_row * local_col, posterior * local_col * local_col])
            moment_acc = moment_acc.at[:, candidate_ids].add(moment_terms)
            return ((count_acc, moment_acc), None)
        start_acc = (jnp.zeros((gene_total, cell_count), jnp.float32), jnp.zeros((6, cell_count), jnp.float32))
        (gene_counts, moments), _ = lax.scan(tile_row, start_acc, jnp.arange(tile_rows, dtype=jnp.int32))
        profile, centre_row, centre_col, cov_rr, cov_rc, cov_cc, log_weight = update_cells(gene_counts, tuple((moments[member] for member in range(6))), centre_row, centre_col, cov_rr, cov_rc, cov_cc)
    final_profile = jnp.log(profile).reshape(gene_total, tile_rows, tile_cols, tile_cells)
    final_cells = cell_summary(centre_row, centre_col, cov_rr, cov_rc, cov_cc, log_weight)
    return (final_profile, final_cells.reshape(6, tile_rows, tile_cols, tile_cells))
```

```python
import functools

import jax
import jax.numpy as jnp
from jax import lax
from jax.experimental import pallas as pl
from jax.experimental.pallas import tpu as pltpu
from jax.sharding import PartitionSpec as P

ITERS = 2
LANES = 128
NEG = -3.0e38
PIECES = 2
SPAN = 256
STRIP = 32
FINE = 32

pseudo_count = 0.05
prior_weight = 1.0


def count_chunk(cand_ref, first, low, rows_ref, outs):
    slots = cand_ref.shape[1]
    cells = outs[0].shape[0]
    coarse = cells // FINE
    bf16 = jnp.bfloat16
    fine_iota = lax.broadcasted_iota(jnp.int32, (FINE, slots), 0).astype(jnp.float32).astype(bf16)
    coarse_iota = lax.broadcasted_iota(jnp.int32, (16, slots), 0).astype(jnp.float32).astype(bf16)
    one = jnp.ones((), bf16)
    zero = jnp.zeros((), bf16)
    empty = jnp.zeros((16, slots), bf16)

    for start in range(0, LANES, 16):
        ids = cand_ref[pl.ds(pl.multiple_of(first + start, 16), 16), :]
        major = lax.div(ids, jnp.int32(FINE))
        minor = (ids - major * FINE).astype(jnp.float32).astype(bf16)
        major = (major - low).astype(jnp.float32).astype(bf16)
        for t in range(0, 16, 2):
            fine_hot = [jnp.where(fine_iota == minor[u : u + 1, :], one, zero) for u in (t, t + 1)]
            coarse_hot = [jnp.where(coarse_iota == major[u : u + 1, :], one, zero) for u in (t, t + 1)]
            left = jnp.concatenate(
                [
                    jnp.concatenate([coarse_hot[0], empty], axis=1),
                    jnp.concatenate([empty, coarse_hot[1]], axis=1),
                ],
                axis=0,
            )
            rows_ref[(start + t) * 16 : (start + t) * 16 + 32, 0:FINE] = lax.dot_general(
                left,
                jnp.concatenate(fine_hot, axis=1),
                (((1,), (1,)), ((), ())),
                preferred_element_type=jnp.float32,
            )

    for a in range(3):
        outs[a][...] = jnp.concatenate(
            [rows_ref[pl.ds(a * coarse + h, LANES, stride=16), 0:FINE].T for h in range(coarse)], axis=0
        )


def em_kernel(
    rows, cols, live_ref, cand_ref, pos_ref, gene_ref, w_ref, cent_ref, spread_ref, corr_ref, prof_out, cells_out,
    rows_ref, cand_all, m_send, m_all, tok_ref, logs_ref, tok_all, e_all, hot, table, gl, par, state, acc, share,
    stat_send, stat_recv, fac_send, fac_recv,
    cs_sem, cr_sem, ms_sem, mr_sem, ts_sem, tr_sem, ss_sem, sr_sem, fs_sem, fr_sem,
):
    genes, cells = w_ref.shape
    gene_pad = hot.shape[0]
    tokens = tok_ref.shape[1]
    chunks = tokens // LANES
    my_row = lax.axis_index("row")
    my_col = lax.axis_index("col")

    def offsets(b):
        return b // 3 - 1, b % 3 - 1

    def at(b, c):
        return pl.ds(pl.multiple_of(b * tokens + c * LANES, LANES), LANES)

    def exists(b):
        dr, dc = offsets(b)
        r, c = my_row + dr, my_col + dc
        return (r >= 0) & (r < rows) & (c >= 0) & (c < cols)

    def place(b):
        dr, dc = offsets(b)
        return {"row": my_row + dr, "col": my_col + dc}

    def remote(src, dst, send, recv, b):
        return pltpu.make_async_remote_copy(
            src_ref=src, dst_ref=dst, send_sem=send, recv_sem=recv,
            device_id=place(b), device_id_type=pl.DeviceIdType.MESH,
        )

    def send_c(c, side):
        part = pl.ds(pl.multiple_of(c * LANES, LANES), LANES)
        b = 7 if side else 1
        return remote(
            cand_ref.at[part], cand_all.at[1 - side, part], cs_sem.at[c, side], cr_sem.at[c, 1 - side], b
        )

    def recv_c(c, side):
        part = pl.ds(pl.multiple_of(c * LANES, LANES), LANES)
        b = 7 if side else 1
        return remote(
            cand_ref.at[part], cand_all.at[side, part], cs_sem.at[c, 1 - side], cr_sem.at[c, side], b
        )

    def across(b):
        return b + 2 - 2 * (b % 3)

    def column_place(b):
        return {"col": my_col + b % 3 - 1}

    def send_m(c, b):
        return pltpu.make_async_remote_copy(
            src_ref=m_send.at[c, b], dst_ref=m_all.at[c, across(b)],
            send_sem=ms_sem.at[c, b], recv_sem=mr_sem.at[c, across(b)],
            device_id=column_place(b), device_id_type=pl.DeviceIdType.MESH,
        )

    def recv_m(c, b):
        return pltpu.make_async_remote_copy(
            src_ref=m_send.at[c, across(b)], dst_ref=m_all.at[c, b],
            send_sem=ms_sem.at[c, across(b)], recv_sem=mr_sem.at[c, b],
            device_id=column_place(b), device_id_type=pl.DeviceIdType.MESH,
        )

    def send_t(b):
        return remote(tok_ref, tok_all.at[8 - b], ts_sem.at[b], tr_sem.at[8 - b], b)

    def recv_t(b):
        return remote(tok_ref, tok_all.at[b], ts_sem.at[8 - b], tr_sem.at[b], b)

    def send_s(it, b):
        return remote(stat_send.at[it, b], stat_recv.at[it, 8 - b], ss_sem.at[it, b], sr_sem.at[it, 8 - b], b)

    def recv_s(it, b):
        return remote(stat_send.at[it, 8 - b], stat_recv.at[it, b], ss_sem.at[it, 8 - b], sr_sem.at[it, b], b)

    def send_f(it, b):
        return remote(fac_send.at[it, b], fac_recv.at[it, 8 - b], fs_sem.at[it, b], fr_sem.at[it, 8 - b], b)

    def recv_f(it, b):
        return remote(fac_send.at[it, 8 - b], fac_recv.at[it, b], fs_sem.at[it, 8 - b], fr_sem.at[it, b], b)

    others = (1, 7, 0, 2, 6, 8, 3, 5)
    barrier = pltpu.get_barrier_semaphore()
    near = 0
    for b in others:
        near = near + exists(b).astype(jnp.int32)

        @pl.when(exists(b))
        def _():
            pl.semaphore_signal(barrier, inc=1, device_id=place(b), device_id_type=pl.DeviceIdType.MESH)

    tok_ref[0:1, :] = pos_ref[0, 0]
    tok_ref[1:2, :] = pos_ref[1, 0]
    tok_ref[2:3, :] = gene_ref[0].astype(jnp.float32)
    blocks = live_ref.shape[2]
    block = tokens // blocks
    for n in range(blocks):
        inside = lax.broadcasted_iota(jnp.int32, (1, block), 1) < live_ref[0, 0, n]
        tok_ref[3:4, n * block : (n + 1) * block] = jnp.where(inside, 1.0, 0.0)
    tok_ref[4:8, :] = jnp.zeros((4, tokens), jnp.float32)

    for b in others:

        @pl.when(jnp.logical_not(exists(b)))
        def _():
            hot[:, b * tokens : (b + 1) * tokens] = jnp.zeros((gene_pad, tokens), jnp.bfloat16)
            share[:, b * tokens : (b + 1) * tokens] = jnp.zeros((cells, tokens), jnp.bfloat16)
            for it in range(ITERS):
                stat_recv[it, b, 0:1, :] = jnp.full((1, tokens), NEG, jnp.float32)
                stat_recv[it, b, 1:2, :] = jnp.zeros((1, tokens), jnp.float32)

    wide = (cells, LANES)
    acc[0] = jnp.zeros(wide, jnp.float32)
    acc[0, 0:1, :] = cent_ref[0, 0]
    acc[0, 1:2, :] = cent_ref[1, 0]
    acc[0, 2:3, :] = spread_ref[0, 0]
    acc[0, 3:4, :] = spread_ref[1, 0]
    acc[0, 4:5, :] = corr_ref[0]
    initial = acc[0].T

    def column(j):
        return jnp.broadcast_to(initial[:, j : j + 1], wide)

    sd_row, sd_col = column(2), column(3)
    state[0] = column(0)
    state[1] = column(1)
    state[2] = sd_row * sd_row
    state[3] = column(4) * sd_row * sd_col
    state[4] = sd_col * sd_col
    state[5] = jnp.zeros(wide, jnp.float32)
    weights = w_ref[...]
    logs_ref[...] = jnp.log(weights / jnp.sum(weights, axis=0, keepdims=True))

    pl.semaphore_wait(barrier, near)
    for side in range(2):
        for c in range(chunks):

            @pl.when(exists(7 if side else 1))
            def _():
                send_c(c, side).start()

    for b in others:

        @pl.when(exists(b))
        def _():
            send_t(b).start()

    coarse = cells // FINE
    for source, list_ref, side in ((1, cand_ref, None), (0, cand_all.at[0], 0), (2, cand_all.at[1], 1)):
        mine = source * 3 + 1

        def count_and_send(c, carry):
            if side is not None:
                recv_c(c, side).wait_recv()
            count_chunk(
                list_ref,
                c * LANES,
                (2 - source) * 3 * coarse,
                rows_ref,
                (m_send.at[c, mine - 1], m_all.at[c, mine], m_send.at[c, mine + 1]),
            )
            for b in (mine - 1, mine + 1):

                @pl.when(exists(b - mine + 4))
                def _():
                    send_m(c, b).start()

            return carry

        if side is None:
            lax.fori_loop(0, chunks, count_and_send, 0)
        else:

            @pl.when(exists(mine))
            def _():
                lax.fori_loop(0, chunks, count_and_send, 0)

    def in_order(k):
        step = (k + 1) // 2
        return 4 + (step + (step == 1) * 2 - (step == 2) - (step == 3)) * (2 * (k % 2) - 1)

    for it in range(ITERS):
        c00, c01, c11 = state[2], state[3], state[4]
        det = c00 * c11 - c01 * c01
        par[0] = 0.5 * (c11 / det)
        par[1] = -c01 / det
        par[2] = 0.5 * (c00 / det)
        par[3] = state[5] - 0.5 * jnp.log(det)
        logs = logs_ref[...]
        if gene_pad > genes:
            logs = jnp.concatenate([logs, jnp.zeros((gene_pad - genes, cells), jnp.float32)], axis=0)
        logs = logs.T
        for piece in range(PIECES):
            part = logs.astype(jnp.bfloat16)
            table[piece * cells : (piece + 1) * cells, :] = part
            logs = logs - part.astype(jnp.float32)

        gene_iota = (
            lax.broadcasted_iota(jnp.int32, (min(SPAN, gene_pad), LANES), 0)
            .astype(jnp.float32)
            .astype(jnp.bfloat16)
        )
        hot_one = jnp.ones((), jnp.bfloat16)
        hot_zero = jnp.zeros((), jnp.bfloat16)

        def score_tile(k, carry):
            b = in_order(k)
            dr, dc = offsets(b)

            @pl.when(exists(b))
            def _():
                if it == 0:

                    @pl.when(b == 4)
                    def _():
                        tok_all[4] = tok_ref[...]

                    @pl.when(b != 4)
                    def _():
                        recv_t(b).wait_recv()

                    for c in range(chunks):
                        lanes = slice(c * LANES, (c + 1) * LANES)
                        ids = tok_all[b, 2:3, lanes]
                        for low in range(0, gene_pad, SPAN):
                            high = min(low + SPAN, gene_pad)
                            here = (ids - float(low)).astype(jnp.bfloat16)
                            same = gene_iota[: high - low] == here
                            hot[low:high, at(b, c)] = jnp.where(same, hot_one, hot_zero)

                gl[...] = jnp.dot(
                    table[...],
                    hot[:, pl.ds(pl.multiple_of(b * tokens, LANES), tokens)],
                    preferred_element_type=jnp.float32,
                )
                for c in range(chunks):
                    if it == 0:

                        @pl.when(b % 3 != 1)
                        def _():
                            recv_m(c, b).wait_recv()

                    lanes = slice(c * LANES, (c + 1) * LANES)
                    y0 = tok_all[b, 0:1, lanes] + dr.astype(jnp.float32)
                    y1 = tok_all[b, 1:2, lanes] + dc.astype(jnp.float32)
                    d0 = y0 - state[0]
                    d1 = y1 - state[1]
                    base = gl[0:cells, lanes]
                    for piece in range(1, PIECES):
                        base = base + gl[piece * cells : (piece + 1) * cells, lanes]
                    score = base + par[3] - (d0 * (par[0] * d0 + par[1] * d1) + par[2] * d1 * d1)
                    times = m_all[c, b]
                    score = jnp.where(times > 0.0, score, NEG)
                    top = jnp.max(score, axis=0, keepdims=True)
                    terms = times * jnp.exp(score - top)
                    e_all[b, :, lanes] = terms
                    stat_send[it, b, 0:1, lanes] = top
                    stat_send[it, b, 1:2, lanes] = jnp.sum(terms, axis=0, keepdims=True)

                @pl.when(b == 4)
                def _():
                    stat_recv[it, 4] = stat_send[it, 4]

                @pl.when(b != 4)
                def _():
                    send_s(it, b).start()

            return carry

        lax.fori_loop(0, 9, score_tile, 0)

        for b in others:

            @pl.when(exists(b))
            def _():
                recv_s(it, b).wait_recv()

        top = stat_recv[it, 4, 0:1, :]
        for b in others:
            top = jnp.maximum(top, stat_recv[it, b, 0:1, :])
        total = jnp.zeros((1, tokens), jnp.float32)
        for b in range(9):
            total = total + stat_recv[it, b, 1:2, :] * jnp.exp(stat_recv[it, b, 0:1, :] - top)
        scale = tok_ref[3:4, :] / total
        fac_recv[it, 4] = scale * jnp.exp(stat_recv[it, 4, 0:1, :] - top)
        for b in others:
            fac_send[it, b] = scale * jnp.exp(stat_recv[it, b, 0:1, :] - top)
        for b in others:

            @pl.when(exists(b))
            def _():
                send_f(it, b).start()

        for j in range(6):
            acc[j] = jnp.zeros(wide, jnp.float32)

        def sum_tile(k, carry):
            b = in_order(k)
            dr, dc = offsets(b)

            @pl.when(exists(b))
            def _():
                @pl.when(b != 4)
                def _():
                    recv_f(it, b).wait_recv()

                for first in range(0, cells, STRIP):
                    strip = slice(first, first + STRIP)
                    sums = None
                    for c in range(chunks):
                        lanes = slice(c * LANES, (c + 1) * LANES)
                        y0 = tok_all[b, 0:1, lanes] + dr.astype(jnp.float32)
                        y1 = tok_all[b, 1:2, lanes] + dc.astype(jnp.float32)
                        post = e_all[b, strip, lanes] * fac_recv[it, b, :, lanes]
                        share[strip, at(b, c)] = post.astype(jnp.bfloat16)
                        by0 = post * y0
                        by1 = post * y1
                        terms = (post, by0, by1, by0 * y0, by0 * y1, by1 * y1)
                        sums = terms if sums is None else tuple(x + y for x, y in zip(sums, terms))
                    for j in range(6):
                        acc[j, strip, :] += sums[j]
            return carry

        lax.fori_loop(0, 9, sum_tile, 0)
        gene_counts = lax.dot_general(
            hot[...], share[...], (((1,), (1,)), ((), ())), preferred_element_type=jnp.float32
        )[0:genes, :]

        mass, s0, s1, s00, s01, s11 = [
            jnp.broadcast_to(jnp.sum(acc[j], axis=1, keepdims=True), wide) for j in range(6)
        ]
        profile = (gene_counts + pseudo_count) / (
            jnp.sum(gene_counts, axis=0, keepdims=True) + genes * pseudo_count
        )
        if it + 1 < ITERS:
            logs_ref[...] = jnp.log(profile)
        else:
            prof_out[...] = profile
        below = mass + prior_weight
        mu0 = (s0 + prior_weight * state[0]) / below
        mu1 = (s1 + prior_weight * state[1]) / below
        q00 = s00 - 2.0 * mu0 * s0 + mass * mu0 * mu0
        q01 = s01 - mu0 * s1 - mu1 * s0 + mass * mu0 * mu1
        q11 = s11 - 2.0 * mu1 * s1 + mass * mu1 * mu1
        state[0] = mu0
        state[1] = mu1
        state[2] = (q00 + prior_weight * state[2]) / below
        state[3] = (q01 + prior_weight * state[3]) / below
        state[4] = (q11 + prior_weight * state[4]) / below
        state[5] = jnp.log(mass + 1.0)

    fields = (
        state[0],
        state[1],
        0.5 * jnp.log(state[2]),
        0.5 * jnp.log(state[4]),
        state[3] / jnp.sqrt(state[2] * state[4]),
        state[5],
    )
    lane = lax.broadcasted_iota(jnp.int32, wide, 1)
    packed = jnp.zeros(wide, jnp.float32)
    for j, field in enumerate(fields):
        packed = jnp.where(lane == j, field, packed)
    cells_out[...] = packed.T[0:8, :]

    for b in others:

        @pl.when(exists(b))
        def _():
            send_t(b).wait_send()
            for it in range(ITERS):
                send_s(it, b).wait_send()
                send_f(it, b).wait_send()

    for source in range(3):
        for b in (source * 3, source * 3 + 2):

            @pl.when(exists(source * 3 + 1) & exists(b - source * 3 + 3))
            def _():
                for c in range(chunks):
                    send_m(c, b).wait_send()

    for side in range(2):

        @pl.when(exists(7 if side else 1))
        def _():
            for c in range(chunks):
                send_c(c, side).wait_send()


def run_em(rows, cols, live, cand, positions, gene_ids, weights, centroids, spreads, correlation):
    genes, cells = weights.shape
    tokens, slots = cand.shape
    chunks = tokens // LANES
    gene_pad = -(-genes // LANES) * LANES
    f32 = jnp.float32
    dma = pltpu.SemaphoreType.DMA
    return pl.pallas_call(
        functools.partial(em_kernel, rows, cols),
        in_specs=[pl.BlockSpec(memory_space=pltpu.SMEM)] + [pl.BlockSpec(memory_space=pltpu.VMEM)] * 7,
        out_specs=[pl.BlockSpec(memory_space=pltpu.VMEM)] * 2,
        out_shape=(
            jax.ShapeDtypeStruct((genes, cells), f32),
            jax.ShapeDtypeStruct((8, cells), f32),
        ),
        scratch_shapes=[
            pltpu.VMEM((LANES * 16, cells), f32),
            pltpu.VMEM((2, tokens, slots), jnp.int32),
            pltpu.VMEM((chunks, 9, cells, LANES), f32),
            pltpu.VMEM((chunks, 9, cells, LANES), f32),
            pltpu.VMEM((8, tokens), f32),
            pltpu.VMEM((genes, cells), f32),
            pltpu.VMEM((9, 8, tokens), f32),
            pltpu.VMEM((9, cells, tokens), f32),
            pltpu.VMEM((gene_pad, 9 * tokens), jnp.bfloat16),
            pltpu.VMEM((PIECES * cells, gene_pad), jnp.bfloat16),
            pltpu.VMEM((PIECES * cells, tokens), f32),
            pltpu.VMEM((4, cells, LANES), f32),
            pltpu.VMEM((6, cells, LANES), f32),
            pltpu.VMEM((6, cells, LANES), f32),
            pltpu.VMEM((cells, 9 * tokens), jnp.bfloat16),
            pltpu.VMEM((ITERS, 9, 2, tokens), f32),
            pltpu.VMEM((ITERS, 9, 2, tokens), f32),
            pltpu.VMEM((ITERS, 9, 1, tokens), f32),
            pltpu.VMEM((ITERS, 9, 1, tokens), f32),
            dma((chunks, 2)),
            dma((chunks, 2)),
            dma((chunks, 9)),
            dma((chunks, 9)),
            dma((9,)),
            dma((9,)),
            dma((ITERS, 9)),
            dma((ITERS, 9)),
            dma((ITERS, 9)),
            dma((ITERS, 9)),
        ],
        compiler_params=pltpu.CompilerParams(collective_id=0, has_side_effects=True),
        name="em_cells",
    )(live, cand, positions, gene_ids, weights, centroids, spreads, correlation)


def body(
    rows, cols, positions, genes, candidates, block_counts, profile_weights, centroids, spreads, correlation
):
    profile, summary = run_em(
        rows,
        cols,
        block_counts,
        candidates[0, 0],
        positions,
        genes,
        profile_weights[:, 0, 0, :],
        centroids,
        spreads,
        correlation,
    )
    return (jnp.log(profile)[:, None, None, :], summary[:6][:, None, None, :])


def solution(mesh):
    return jax.shard_map(
        functools.partial(body, mesh.shape["row"], mesh.shape["col"]),
        mesh=mesh,
        in_specs=(
            P(None, ("groups", "row"), "col", None),
            P(("groups", "row"), "col", None),
            P(("groups", "row"), "col", None, None),
            P(("groups", "row"), "col", None),
            P(None, ("groups", "row"), "col", None),
            P(None, ("groups", "row"), "col", None),
            P(None, ("groups", "row"), "col", None),
            P(("groups", "row"), "col", None),
        ),
        out_specs=(
            P(None, ("groups", "row"), "col", None),
            P(None, ("groups", "row"), "col", None),
        ),
        check_vma=False,
    )
```

```python
import functools

import jax
import jax.numpy as jnp
from jax import lax
from jax.experimental import pallas as pl
from jax.experimental.pallas import tpu as pltpu
from jax.sharding import PartitionSpec as P

ITERS = 2
LANES = 128
NEG = -3.0e38
PIECES = 2
SPAN = 256
STRIP = 32
FINE = 32
PITCH = 17
LOG2E = 1.4426950408889634
EARLY = (4, 3, 5, 1, 7, 0, 2, 6, 8)
LATE = (0, 2, 6, 8, 1, 7, 3, 5, 4)

pseudo_count = 0.05
prior_weight = 1.0


def pick(order, k):
    if isinstance(k, int):
        return order[k]
    return sum(jnp.where(k == i, b, 0) for i, b in enumerate(order))


def log_profile(gene_counts):
    total = jnp.sum(gene_counts, axis=0, keepdims=True) + gene_counts.shape[0] * pseudo_count
    return jnp.log(gene_counts + pseudo_count) - jnp.log(total)


def count_chunk(cand_ref, first, low, rows_ref, outs):
    slots = cand_ref.shape[1]
    cells = outs[0].shape[0]
    coarse = cells // FINE
    bf16 = jnp.bfloat16
    fine_iota = lax.broadcasted_iota(jnp.int32, (FINE, slots), 0).astype(jnp.float32).astype(bf16)
    coarse_iota = lax.broadcasted_iota(jnp.int32, (16, slots), 0).astype(jnp.float32).astype(bf16)
    one = jnp.ones((), bf16)
    zero = jnp.zeros((), bf16)
    empty = jnp.zeros((16, slots), bf16)

    for start in range(0, LANES, 16):
        ids = cand_ref[pl.ds(pl.multiple_of(first + start, 16), 16), :]
        major = lax.div(ids, jnp.int32(FINE))
        minor = (ids - major * FINE).astype(jnp.float32).astype(bf16)
        major = (major - low).astype(jnp.float32).astype(bf16)
        for t in range(0, 16, 2):
            fine_hot = [jnp.where(fine_iota == minor[u : u + 1, :], one, zero) for u in (t, t + 1)]
            coarse_hot = [jnp.where(coarse_iota == major[u : u + 1, :], one, zero) for u in (t, t + 1)]
            left = jnp.concatenate(
                [
                    jnp.concatenate([coarse_hot[0], empty], axis=1),
                    jnp.concatenate([empty, coarse_hot[1]], axis=1),
                ],
                axis=0,
            )
            times = lax.dot_general(
                left,
                jnp.concatenate(fine_hot, axis=1),
                (((1,), (1,)), ((), ())),
                preferred_element_type=jnp.float32,
            )
            for u in (0, 1):
                row = (start + t + u) * PITCH
                rows_ref[row : row + 16, 0:FINE] = times[u * 16 : u * 16 + 16]

    for a in range(3):
        outs[a][...] = jnp.concatenate(
            [rows_ref[pl.ds(a * coarse + h, LANES, stride=PITCH), 0:FINE].T for h in range(coarse)], axis=0
        )


def em_kernel(
    rows, cols, live_ref, cand_ref, pos_ref, gene_ref, w_ref, cent_ref, spread_ref, corr_ref, counts, cells_out,
    rows_ref, cand_all, m_send, m_all, tok_ref, tok_all, e_all, hot, table, gl_a, gl_b, par, state, acc, share_a, share_b,
    stat_send, stat_recv, fac_send, fac_recv,
    cs_sem, cr_sem, ms_sem, mr_sem, ts_sem, tr_sem, ss_sem, sr_sem, fs_sem, fr_sem,
):
    genes, cells = w_ref.shape
    gene_pad = hot.shape[0]
    tokens = tok_ref.shape[1]
    chunks = tokens // LANES
    my_row = lax.axis_index("row")
    my_col = lax.axis_index("col")

    def offsets(b):
        return b // 3 - 1, b % 3 - 1

    def at(b, c):
        return pl.ds(pl.multiple_of(b * tokens + c * LANES, LANES), LANES)

    def exists(b):
        dr, dc = offsets(b)
        r, c = my_row + dr, my_col + dc
        return (r >= 0) & (r < rows) & (c >= 0) & (c < cols)

    def place(b):
        dr, dc = offsets(b)
        return {"row": my_row + dr, "col": my_col + dc}

    def remote(src, dst, send, recv, b):
        return pltpu.make_async_remote_copy(
            src_ref=src, dst_ref=dst, send_sem=send, recv_sem=recv,
            device_id=place(b), device_id_type=pl.DeviceIdType.MESH,
        )

    def send_c(c, side):
        part = pl.ds(pl.multiple_of(c * LANES, LANES), LANES)
        b = 7 if side else 1
        return remote(
            cand_ref.at[part], cand_all.at[1 - side, part], cs_sem.at[c, side], cr_sem.at[c, 1 - side], b
        )

    def recv_c(c, side):
        part = pl.ds(pl.multiple_of(c * LANES, LANES), LANES)
        b = 7 if side else 1
        return remote(
            cand_ref.at[part], cand_all.at[side, part], cs_sem.at[c, 1 - side], cr_sem.at[c, side], b
        )

    def across(b):
        return b + 2 - 2 * (b % 3)

    def column_place(b):
        return {"col": my_col + b % 3 - 1}

    def send_m(c, b):
        return pltpu.make_async_remote_copy(
            src_ref=m_send.at[c, b], dst_ref=m_all.at[c, across(b)],
            send_sem=ms_sem.at[c, b], recv_sem=mr_sem.at[c, across(b)],
            device_id=column_place(b), device_id_type=pl.DeviceIdType.MESH,
        )

    def recv_m(c, b):
        return pltpu.make_async_remote_copy(
            src_ref=m_send.at[c, across(b)], dst_ref=m_all.at[c, b],
            send_sem=ms_sem.at[c, across(b)], recv_sem=mr_sem.at[c, b],
            device_id=column_place(b), device_id_type=pl.DeviceIdType.MESH,
        )

    def send_t(b):
        return remote(tok_ref, tok_all.at[8 - b], ts_sem.at[b], tr_sem.at[8 - b], b)

    def recv_t(b):
        return remote(tok_ref, tok_all.at[b], ts_sem.at[8 - b], tr_sem.at[b], b)

    def send_s(it, b):
        return remote(stat_send.at[it, b], stat_recv.at[it, 8 - b], ss_sem.at[it, b], sr_sem.at[it, 8 - b], b)

    def recv_s(it, b):
        return remote(stat_send.at[it, 8 - b], stat_recv.at[it, b], ss_sem.at[it, 8 - b], sr_sem.at[it, b], b)

    def send_f(it, b):
        return remote(fac_send.at[it, b], fac_recv.at[it, 8 - b], fs_sem.at[it, b], fr_sem.at[it, 8 - b], b)

    def recv_f(it, b):
        return remote(fac_send.at[it, 8 - b], fac_recv.at[it, b], fs_sem.at[it, 8 - b], fr_sem.at[it, b], b)

    others = (1, 7, 0, 2, 6, 8, 3, 5)
    barrier = pltpu.get_barrier_semaphore()
    near = 0
    for b in others:
        near = near + exists(b).astype(jnp.int32)

        @pl.when(exists(b))
        def _():
            pl.semaphore_signal(barrier, inc=1, device_id=place(b), device_id_type=pl.DeviceIdType.MESH)

    tok_ref[0:1, :] = pos_ref[0, 0]
    tok_ref[1:2, :] = pos_ref[1, 0]
    tok_ref[2:3, :] = gene_ref[0].astype(jnp.float32)
    blocks = live_ref.shape[2]
    block = tokens // blocks
    for n in range(blocks):
        inside = lax.broadcasted_iota(jnp.int32, (1, block), 1) < live_ref[0, 0, n]
        tok_ref[3:4, n * block : (n + 1) * block] = jnp.where(inside, 1.0, 0.0)
    tok_ref[4:8, :] = jnp.zeros((4, tokens), jnp.float32)

    for b in others:

        @pl.when(jnp.logical_not(exists(b)))
        def _():
            tok_all[b] = jnp.zeros((8, tokens), jnp.float32)
            for c in range(chunks):
                m_all[c, b] = jnp.zeros((cells, LANES), jnp.float32)
            for it in range(ITERS):
                stat_recv[it, b, 0:1, :] = jnp.full((1, tokens), NEG, jnp.float32)
                stat_recv[it, b, 1:2, :] = jnp.zeros((1, tokens), jnp.float32)
                fac_recv[it, b] = jnp.zeros((1, tokens), jnp.float32)

    wide = (cells, LANES)
    acc[0] = jnp.zeros(wide, jnp.float32)
    acc[0, 0:1, :] = cent_ref[0, 0]
    acc[0, 1:2, :] = cent_ref[1, 0]
    acc[0, 2:3, :] = spread_ref[0, 0]
    acc[0, 3:4, :] = spread_ref[1, 0]
    acc[0, 4:5, :] = corr_ref[0]
    initial = acc[0].T

    def column(j):
        return jnp.broadcast_to(initial[:, j : j + 1], wide)

    sd_row, sd_col = column(2), column(3)
    state[0] = column(0)
    state[1] = column(1)
    state[2] = sd_row * sd_row
    state[3] = column(4) * sd_row * sd_col
    state[4] = sd_col * sd_col
    state[5] = jnp.zeros(wide, jnp.float32)

    def fill_table(logs):
        c00, c01, c11 = state[2], state[3], state[4]
        det = c00 * c11 - c01 * c01
        par[0] = (0.5 * LOG2E) * (c11 / det)
        par[1] = -LOG2E * (c01 / det)
        par[2] = (0.5 * LOG2E) * (c00 / det)
        bias = state[5] - 0.5 * jnp.log(det)
        if gene_pad > genes:
            logs = jnp.concatenate([logs, jnp.zeros((gene_pad - genes, cells), jnp.float32)], axis=0)
        for first in range(0, gene_pad, LANES):
            part = (logs[first : first + LANES].T + bias) * LOG2E
            for piece in range(PIECES):
                rounded = part.astype(jnp.bfloat16)
                table[piece * cells : (piece + 1) * cells, first : first + LANES] = rounded
                part = part - rounded.astype(jnp.float32)

    weights = w_ref[...]
    fill_table(jnp.log(weights) - jnp.log(jnp.sum(weights, axis=0, keepdims=True)))

    coarse = cells // FINE

    def count(c, source, list_ref):
        mine = source * 3 + 1
        count_chunk(
            list_ref,
            c * LANES,
            (2 - source) * 3 * coarse,
            rows_ref,
            (m_send.at[c, mine - 1], m_all.at[c, mine], m_send.at[c, mine + 1]),
        )

    def send_counts(c, source):
        for b in (source * 3, source * 3 + 2):

            @pl.when(exists(3 + b % 3))
            def _():
                send_m(c, b).start()

    def count_own(c, carry):
        count(c, 1, cand_ref)

        @pl.when(c == 0)
        def _():
            pl.semaphore_wait(barrier, near)
            for b in others:

                @pl.when(exists(b))
                def _():
                    send_t(b).start()

            for part in range(chunks):
                for side in range(2):

                    @pl.when(exists(7 if side else 1))
                    def _():
                        send_c(part, side).start()

        send_counts(c, 1)
        return carry

    lax.fori_loop(0, chunks, count_own, 0)

    gene_iota = (
        lax.broadcasted_iota(jnp.int32, (min(SPAN, gene_pad), LANES), 0)
        .astype(jnp.float32)
        .astype(jnp.bfloat16)
    )
    hot_one = jnp.ones((), jnp.bfloat16)
    hot_zero = jnp.zeros((), jnp.bfloat16)
    tok_all[4] = tok_ref[...]

    def fill_hot(k, carry):
        b = pick(EARLY, k)

        @pl.when(exists(b) & (b != 4))
        def _():
            recv_t(b).wait_recv()

        for c in range(chunks):
            ids = tok_all[b, 2:3, c * LANES : (c + 1) * LANES]
            for low in range(0, gene_pad, SPAN):
                high = min(low + SPAN, gene_pad)
                here = (ids - float(low)).astype(jnp.bfloat16)
                hot[low:high, at(b, c)] = jnp.where(gene_iota[: high - low] == here, hot_one, hot_zero)
        return carry

    lax.fori_loop(0, 9, fill_hot, 0)

    def count_lists(c, carry):
        for side, source in ((0, 0), (1, 2)):

            @pl.when(exists(source * 3 + 1))
            def _():
                recv_c(c, side).wait_recv()
                count(c, source, cand_all.at[side])
                send_counts(c, source)

        return carry

    lax.fori_loop(0, chunks, count_lists, 0)

    def hot_of(b):
        return hot[:, pl.ds(pl.multiple_of(b * tokens, LANES), tokens)]

    for it in range(ITERS):
        order = EARLY if it == 0 else LATE

        def look_up(k, gl):
            gl[...] = jnp.dot(table[...], hot_of(pick(order, k)), preferred_element_type=jnp.float32)

        def score_tile(k, gl, ahead):
            b = pick(order, k)
            dr, dc = offsets(b)
            if it == 0:

                @pl.when(exists(b) & (b % 3 != 1))
                def _():
                    for c in range(chunks):
                        recv_m(c, b).wait_recv()

            if ahead is not None:
                look_up(k + 1, ahead)
            each = [slice(c * LANES, (c + 1) * LANES) for c in range(chunks)]
            y0 = [tok_all[b, 0:1, lanes] + jnp.asarray(dr, jnp.float32) for lanes in each]
            y1 = [tok_all[b, 1:2, lanes] + jnp.asarray(dc, jnp.float32) for lanes in each]
            tops = [jnp.full((8, LANES), NEG, jnp.float32) for _ in each]
            for first in range(0, cells, 8):
                strip = slice(first, first + 8)
                mu0, mu1 = state[0, strip], state[1, strip]
                p00, p01, p11 = par[0, strip], par[1, strip], par[2, strip]
                for c, lanes in enumerate(each):
                    d0 = y0[c] - mu0
                    d1 = y1[c] - mu1
                    base = gl[strip, lanes]
                    for piece in range(1, PIECES):
                        base = base + gl[piece * cells + first : piece * cells + first + 8, lanes]
                    score = base - (d0 * (p00 * d0 + p01 * d1) + p11 * d1 * d1)
                    score = jnp.where(m_all[c, b, strip] > 0.0, score, NEG)
                    tops[c] = jnp.maximum(tops[c], score)
                    e_all[b, strip, lanes] = score
            tops = [jnp.max(top, axis=0, keepdims=True) for top in tops]
            sums = [jnp.zeros((8, LANES), jnp.float32) for _ in each]
            for first in range(0, cells, 8):
                strip = slice(first, first + 8)
                for c, lanes in enumerate(each):
                    terms = m_all[c, b, strip] * jnp.exp2(e_all[b, strip, lanes] - tops[c])
                    e_all[b, strip, lanes] = terms
                    sums[c] = sums[c] + terms
            for c, lanes in enumerate(each):
                stat_send[it, b, 0:1, lanes] = tops[c]
                stat_send[it, b, 1:2, lanes] = jnp.sum(sums[c], axis=0, keepdims=True)

            @pl.when(exists(b) & (b != 4))
            def _():
                send_s(it, b).start()

        look_up(0, gl_a)

        def score_pair(i, carry):
            score_tile(2 * i, gl_a, gl_b)
            score_tile(2 * i + 1, gl_b, gl_a)
            return carry

        lax.fori_loop(0, 4, score_pair, 0)
        score_tile(8, gl_a, None)

        stat_recv[it, 4] = stat_send[it, 4]
        for b in others:

            @pl.when(exists(b))
            def _():
                recv_s(it, b).wait_recv()

        top = stat_recv[it, 4, 0:1, :]
        for b in others:
            top = jnp.maximum(top, stat_recv[it, b, 0:1, :])
        total = jnp.zeros((1, tokens), jnp.float32)
        for b in range(9):
            total = total + stat_recv[it, b, 1:2, :] * jnp.exp2(stat_recv[it, b, 0:1, :] - top)
        scale = tok_ref[3:4, :] / total
        for b in (0, 2, 6, 8, 1, 7, 3, 5):
            fac_send[it, b] = scale * jnp.exp2(stat_recv[it, b, 0:1, :] - top)

            @pl.when(exists(b))
            def _():
                send_f(it, b).start()

        fac_recv[it, 4] = scale * jnp.exp2(stat_recv[it, 4, 0:1, :] - top)

        for j in range(6):
            acc[j] = jnp.zeros(wide, jnp.float32)
        counts[...] = jnp.zeros(counts.shape, jnp.float32)

        def count_genes(k, share):
            b = pick(EARLY, k)
            for low in range(0, gene_pad, SPAN):
                part = slice(low, min(low + SPAN, gene_pad))
                counts[part, :] += lax.dot_general(
                    hot[part, pl.ds(pl.multiple_of(b * tokens, LANES), tokens)],
                    share[...],
                    (((1,), (1,)), ((), ())),
                    preferred_element_type=jnp.float32,
                )

        def sum_tile(k, share, behind):
            b = pick(EARLY, k)
            dr, dc = offsets(b)

            @pl.when(exists(b) & (b != 4))
            def _():
                recv_f(it, b).wait_recv()

            if behind is not None:
                count_genes(k - 1, behind)
            for first in range(0, cells, STRIP):
                strip = slice(first, first + STRIP)
                sums = None
                for c in range(chunks):
                    lanes = slice(c * LANES, (c + 1) * LANES)
                    y0 = tok_all[b, 0:1, lanes] + jnp.asarray(dr, jnp.float32)
                    y1 = tok_all[b, 1:2, lanes] + jnp.asarray(dc, jnp.float32)
                    post = e_all[b, strip, lanes] * fac_recv[it, b, :, lanes]
                    share[strip, lanes] = post.astype(jnp.bfloat16)
                    by0 = post * y0
                    by1 = post * y1
                    terms = (post, by0, by1, by0 * y0, by0 * y1, by1 * y1)
                    sums = terms if sums is None else tuple(x + y for x, y in zip(sums, terms))
                for j in range(6):
                    acc[j, strip, :] += sums[j]

        sum_tile(0, share_a, None)

        def sum_pair(i, carry):
            sum_tile(2 * i + 1, share_b, share_a)
            sum_tile(2 * i + 2, share_a, share_b)
            return carry

        lax.fori_loop(0, 4, sum_pair, 0)
        count_genes(8, share_a)

        mass, s0, s1, s00, s01, s11 = [
            jnp.broadcast_to(jnp.sum(acc[j], axis=1, keepdims=True), wide) for j in range(6)
        ]
        below = mass + prior_weight
        mu0 = (s0 + prior_weight * state[0]) / below
        mu1 = (s1 + prior_weight * state[1]) / below
        q00 = s00 - 2.0 * mu0 * s0 + mass * mu0 * mu0
        q01 = s01 - mu0 * s1 - mu1 * s0 + mass * mu0 * mu1
        q11 = s11 - 2.0 * mu1 * s1 + mass * mu1 * mu1
        state[0] = mu0
        state[1] = mu1
        state[2] = (q00 + prior_weight * state[2]) / below
        state[3] = (q01 + prior_weight * state[3]) / below
        state[4] = (q11 + prior_weight * state[4]) / below
        state[5] = jnp.log(mass + 1.0)
        if it + 1 < ITERS:
            fill_table(log_profile(counts[0:genes, :]))

    fields = (
        state[0],
        state[1],
        0.5 * jnp.log(state[2]),
        0.5 * jnp.log(state[4]),
        state[3] / jnp.sqrt(state[2] * state[4]),
        state[5],
    )
    lane = lax.broadcasted_iota(jnp.int32, wide, 1)
    packed = jnp.zeros(wide, jnp.float32)
    for j, field in enumerate(fields):
        packed = jnp.where(lane == j, field, packed)
    cells_out[...] = packed.T[0:8, :]

    for b in others:

        @pl.when(exists(b))
        def _():
            send_t(b).wait_send()
            for it in range(ITERS):
                send_s(it, b).wait_send()
                send_f(it, b).wait_send()

    for source in range(3):
        for b in (source * 3, source * 3 + 2):

            @pl.when(exists(source * 3 + 1) & exists(b - source * 3 + 3))
            def _():
                for c in range(chunks):
                    send_m(c, b).wait_send()

    for side in range(2):

        @pl.when(exists(7 if side else 1))
        def _():
            for c in range(chunks):
                send_c(c, side).wait_send()


def run_em(rows, cols, live, cand, positions, gene_ids, weights, centroids, spreads, correlation):
    genes, cells = weights.shape
    tokens, slots = cand.shape
    chunks = tokens // LANES
    gene_pad = -(-genes // LANES) * LANES
    f32 = jnp.float32
    dma = pltpu.SemaphoreType.DMA
    return pl.pallas_call(
        functools.partial(em_kernel, rows, cols),
        in_specs=[pl.BlockSpec(memory_space=pltpu.SMEM)] + [pl.BlockSpec(memory_space=pltpu.VMEM)] * 7,
        out_specs=[pl.BlockSpec(memory_space=pltpu.VMEM)] * 2,
        out_shape=(
            jax.ShapeDtypeStruct((gene_pad, cells), f32),
            jax.ShapeDtypeStruct((8, cells), f32),
        ),
        scratch_shapes=[
            pltpu.VMEM((LANES * PITCH, cells), f32),
            pltpu.VMEM((2, tokens, slots), jnp.int32),
            pltpu.VMEM((chunks, 9, cells, LANES), f32),
            pltpu.VMEM((chunks, 9, cells, LANES), f32),
            pltpu.VMEM((8, tokens), f32),
            pltpu.VMEM((9, 8, tokens), f32),
            pltpu.VMEM((9, cells, tokens), f32),
            pltpu.VMEM((gene_pad, 9 * tokens), jnp.bfloat16),
            pltpu.VMEM((PIECES * cells, gene_pad), jnp.bfloat16),
            pltpu.VMEM((PIECES * cells, tokens), f32),
            pltpu.VMEM((PIECES * cells, tokens), f32),
            pltpu.VMEM((3, cells, LANES), f32),
            pltpu.VMEM((6, cells, LANES), f32),
            pltpu.VMEM((6, cells, LANES), f32),
            pltpu.VMEM((cells, tokens), jnp.bfloat16),
            pltpu.VMEM((cells, tokens), jnp.bfloat16),
            pltpu.VMEM((ITERS, 9, 2, tokens), f32),
            pltpu.VMEM((ITERS, 9, 2, tokens), f32),
            pltpu.VMEM((ITERS, 9, 1, tokens), f32),
            pltpu.VMEM((ITERS, 9, 1, tokens), f32),
            dma((chunks, 2)),
            dma((chunks, 2)),
            dma((chunks, 9)),
            dma((chunks, 9)),
            dma((9,)),
            dma((9,)),
            dma((ITERS, 9)),
            dma((ITERS, 9)),
            dma((ITERS, 9)),
            dma((ITERS, 9)),
        ],
        compiler_params=pltpu.CompilerParams(collective_id=0, has_side_effects=True),
        name="em_cells",
    )(live, cand, positions, gene_ids, weights, centroids, spreads, correlation)


def finish_kernel(counts, summary, prof_out, cells_out):
    prof_out[...] = log_profile(counts[0 : prof_out.shape[0], :])
    for j in range(cells_out.shape[0]):
        cells_out[j, 0] = summary[j : j + 1, :]


def finish(genes, counts, summary):
    cells = counts.shape[1]
    return pl.pallas_call(
        finish_kernel,
        in_specs=[pl.BlockSpec(memory_space=pltpu.VMEM)] * 2,
        out_specs=[pl.BlockSpec(memory_space=pltpu.VMEM)] * 2,
        out_shape=(
            jax.ShapeDtypeStruct((genes, cells), jnp.float32),
            jax.ShapeDtypeStruct((6, 1, 1, cells), jnp.float32),
        ),
        name="finish",
    )(counts, summary)


def body(
    rows, cols, positions, genes, candidates, block_counts, profile_weights, centroids, spreads, correlation
):
    counts, summary = run_em(
        rows,
        cols,
        block_counts,
        candidates[0, 0],
        positions,
        genes,
        profile_weights[:, 0, 0, :],
        centroids,
        spreads,
        correlation,
    )
    profile, cell_rows = finish(profile_weights.shape[0], counts, summary)
    return (profile[:, None, None, :], cell_rows)


def solution(mesh):
    return jax.shard_map(
        functools.partial(body, mesh.shape["row"], mesh.shape["col"]),
        mesh=mesh,
        in_specs=(
            P(None, ("groups", "row"), "col", None),
            P(("groups", "row"), "col", None),
            P(("groups", "row"), "col", None, None),
            P(("groups", "row"), "col", None),
            P(None, ("groups", "row"), "col", None),
            P(None, ("groups", "row"), "col", None),
            P(None, ("groups", "row"), "col", None),
            P(("groups", "row"), "col", None),
        ),
        out_specs=(
            P(None, ("groups", "row"), "col", None),
            P(None, ("groups", "row"), "col", None),
        ),
        check_vma=False,
    )
```

```python
import functools

import jax
import jax.numpy as jnp
from jax import lax
from jax.experimental import pallas as pl
from jax.experimental.pallas import tpu as pltpu
from jax.sharding import PartitionSpec as P

ITERS = 2
LANES = 128
NEG = -3.0e38
PIECES = 2
SPAN = 256
STRIP = 32
FINE = 32
PITCH = 17
LOG2E = 1.4426950408889634
EARLY = (4, 3, 5, 1, 7, 0, 2, 6, 8)
LATE = (0, 2, 6, 8, 1, 7, 3, 5, 4)
FIRST = (3, 5, 1, 7, 0, 2, 6, 8, 4)

pseudo_count = 0.05
prior_weight = 1.0


def pick(order, k):
    if isinstance(k, int):
        return order[k]
    return sum(jnp.where(k == i, b, 0) for i, b in enumerate(order))


def log_profile(gene_counts, genes):
    total = jnp.sum(gene_counts, axis=1, keepdims=True) + genes * pseudo_count
    return jnp.log(gene_counts + pseudo_count) - jnp.log(total)


def count_chunk(cand_ref, first, low, rows_ref, outs):
    slots = cand_ref.shape[1]
    cells = outs[0].shape[0]
    coarse = cells // FINE
    bf16 = jnp.bfloat16
    fine_iota = lax.broadcasted_iota(jnp.int32, (FINE, slots), 0).astype(jnp.float32).astype(bf16)
    coarse_iota = lax.broadcasted_iota(jnp.int32, (16, slots), 0).astype(jnp.float32).astype(bf16)
    one = jnp.ones((), bf16)
    zero = jnp.zeros((), bf16)
    empty = jnp.zeros((16, slots), bf16)

    for start in range(0, LANES, 16):
        ids = cand_ref[pl.ds(pl.multiple_of(first + start, 16), 16), :]
        major = lax.div(ids, jnp.int32(FINE))
        minor = (ids - major * FINE).astype(jnp.float32).astype(bf16)
        major = (major - low).astype(jnp.float32).astype(bf16)
        for t in range(0, 16, 2):
            fine_hot = [jnp.where(fine_iota == minor[u : u + 1, :], one, zero) for u in (t, t + 1)]
            coarse_hot = [jnp.where(coarse_iota == major[u : u + 1, :], one, zero) for u in (t, t + 1)]
            left = jnp.concatenate(
                [
                    jnp.concatenate([coarse_hot[0], empty], axis=1),
                    jnp.concatenate([empty, coarse_hot[1]], axis=1),
                ],
                axis=0,
            )
            times = lax.dot_general(
                left,
                jnp.concatenate(fine_hot, axis=1),
                (((1,), (1,)), ((), ())),
                preferred_element_type=jnp.float32,
            )
            for u in (0, 1):
                row = (start + t + u) * PITCH
                rows_ref[row : row + 16, 0:FINE] = times[u * 16 : u * 16 + 16]

    for a in range(3):
        outs[a][...] = jnp.concatenate(
            [rows_ref[pl.ds(a * coarse + h, LANES, stride=PITCH), 0:FINE].T for h in range(coarse)], axis=0
        )


def em_kernel(
    rows, cols, live_ref, cand_ref, pos_ref, gene_ref, w_ref, cent_ref, spread_ref, corr_ref, counts, cells_out,
    rows_ref, cand_all, m_send, m_all, tok_ref, tok_all, e_all, hot, hot_rows, table, gl_a, gl_b, par, state, acc, share_a, share_b,
    stat_send, stat_recv, fac_send, fac_recv,
    cs_sem, cr_sem, ms_sem, mr_sem, ts_sem, tr_sem, ss_sem, sr_sem, fs_sem, fr_sem,
):
    genes, cells = w_ref.shape
    gene_pad = hot.shape[0]
    tokens = tok_ref.shape[1]
    chunks = tokens // LANES
    my_row = lax.axis_index("row")
    my_col = lax.axis_index("col")

    def offsets(b):
        return b // 3 - 1, b % 3 - 1

    def at(b, c):
        return pl.ds(pl.multiple_of(b * tokens + c * LANES, LANES), LANES)

    def exists(b):
        dr, dc = offsets(b)
        r, c = my_row + dr, my_col + dc
        return (r >= 0) & (r < rows) & (c >= 0) & (c < cols)

    def place(b):
        dr, dc = offsets(b)
        return {"row": my_row + dr, "col": my_col + dc}

    def remote(src, dst, send, recv, b):
        return pltpu.make_async_remote_copy(
            src_ref=src, dst_ref=dst, send_sem=send, recv_sem=recv,
            device_id=place(b), device_id_type=pl.DeviceIdType.MESH,
        )

    def send_c(c, side):
        part = pl.ds(pl.multiple_of(c * LANES, LANES), LANES)
        b = 7 if side else 1
        return remote(
            cand_ref.at[part], cand_all.at[1 - side, part], cs_sem.at[c, side], cr_sem.at[c, 1 - side], b
        )

    def recv_c(c, side):
        part = pl.ds(pl.multiple_of(c * LANES, LANES), LANES)
        b = 7 if side else 1
        return remote(
            cand_ref.at[part], cand_all.at[side, part], cs_sem.at[c, 1 - side], cr_sem.at[c, side], b
        )

    def across(b):
        return b + 2 - 2 * (b % 3)

    def column_place(b):
        return {"col": my_col + b % 3 - 1}

    def send_m(c, b):
        return pltpu.make_async_remote_copy(
            src_ref=m_send.at[c, b], dst_ref=m_all.at[c, across(b)],
            send_sem=ms_sem.at[c, b], recv_sem=mr_sem.at[c, across(b)],
            device_id=column_place(b), device_id_type=pl.DeviceIdType.MESH,
        )

    def recv_m(c, b):
        return pltpu.make_async_remote_copy(
            src_ref=m_send.at[c, across(b)], dst_ref=m_all.at[c, b],
            send_sem=ms_sem.at[c, across(b)], recv_sem=mr_sem.at[c, b],
            device_id=column_place(b), device_id_type=pl.DeviceIdType.MESH,
        )

    def send_t(b):
        return remote(tok_ref, tok_all.at[8 - b], ts_sem.at[b], tr_sem.at[8 - b], b)

    def recv_t(b):
        return remote(tok_ref, tok_all.at[b], ts_sem.at[8 - b], tr_sem.at[b], b)

    def send_s(it, b):
        return remote(stat_send.at[it, b], stat_recv.at[it, 8 - b], ss_sem.at[it, b], sr_sem.at[it, 8 - b], b)

    def recv_s(it, b):
        return remote(stat_send.at[it, 8 - b], stat_recv.at[it, b], ss_sem.at[it, 8 - b], sr_sem.at[it, b], b)

    def send_f(it, b):
        return remote(fac_send.at[it, b], fac_recv.at[it, 8 - b], fs_sem.at[it, b], fr_sem.at[it, 8 - b], b)

    def recv_f(it, b):
        return remote(fac_send.at[it, 8 - b], fac_recv.at[it, b], fs_sem.at[it, 8 - b], fr_sem.at[it, b], b)

    others = (1, 7, 0, 2, 6, 8, 3, 5)
    barrier = pltpu.get_barrier_semaphore()
    near = 0
    for b in others:
        near = near + exists(b).astype(jnp.int32)

        @pl.when(exists(b))
        def _():
            pl.semaphore_signal(barrier, inc=1, device_id=place(b), device_id_type=pl.DeviceIdType.MESH)

    tok_ref[0:1, :] = pos_ref[0, 0]
    tok_ref[1:2, :] = pos_ref[1, 0]
    tok_ref[2:3, :] = gene_ref[0].astype(jnp.float32)
    blocks = live_ref.shape[2]
    block = tokens // blocks
    for n in range(blocks):
        inside = lax.broadcasted_iota(jnp.int32, (1, block), 1) < live_ref[0, 0, n]
        tok_ref[3:4, n * block : (n + 1) * block] = jnp.where(inside, 1.0, 0.0)
    tok_ref[4:8, :] = jnp.zeros((4, tokens), jnp.float32)

    for b in others:

        @pl.when(jnp.logical_not(exists(b)))
        def _():
            tok_all[b] = jnp.zeros((8, tokens), jnp.float32)
            for c in range(chunks):
                m_all[c, b] = jnp.zeros((cells, LANES), jnp.float32)
            for it in range(ITERS):
                stat_recv[it, b, 0:1, :] = jnp.full((1, tokens), NEG, jnp.float32)
                stat_recv[it, b, 1:2, :] = jnp.zeros((1, tokens), jnp.float32)
                fac_recv[it, b] = jnp.zeros((1, tokens), jnp.float32)

    wide = (cells, LANES)
    acc[0] = jnp.zeros(wide, jnp.float32)
    acc[0, 0:1, :] = cent_ref[0, 0]
    acc[0, 1:2, :] = cent_ref[1, 0]
    acc[0, 2:3, :] = spread_ref[0, 0]
    acc[0, 3:4, :] = spread_ref[1, 0]
    acc[0, 4:5, :] = corr_ref[0]
    initial = acc[0].T

    def column(j):
        return jnp.broadcast_to(initial[:, j : j + 1], wide)

    sd_row, sd_col = column(2), column(3)
    state[0] = column(0)
    state[1] = column(1)
    state[2] = sd_row * sd_row
    state[3] = column(4) * sd_row * sd_col
    state[4] = sd_col * sd_col
    state[5] = jnp.zeros(wide, jnp.float32)

    def fill_table(logs):
        c00, c01, c11 = state[2], state[3], state[4]
        det = c00 * c11 - c01 * c01
        par[0] = (0.5 * LOG2E) * (c11 / det)
        par[1] = -LOG2E * (c01 / det)
        par[2] = (0.5 * LOG2E) * (c00 / det)
        bias = state[5] - 0.5 * jnp.log(det)
        for first in range(0, gene_pad, LANES):
            part = (logs[:, first : first + LANES] + bias) * LOG2E
            for piece in range(PIECES):
                rounded = part.astype(jnp.bfloat16)
                table[piece * cells : (piece + 1) * cells, first : first + LANES] = rounded
                part = part - rounded.astype(jnp.float32)

    weights = w_ref[...]
    logs = jnp.log(weights) - jnp.log(jnp.sum(weights, axis=0, keepdims=True))
    if gene_pad > genes:
        logs = jnp.concatenate([logs, jnp.zeros((gene_pad - genes, cells), jnp.float32)], axis=0)
    fill_table(logs.T)

    coarse = cells // FINE

    def count(c, source, list_ref):
        mine = source * 3 + 1
        count_chunk(
            list_ref,
            c * LANES,
            (2 - source) * 3 * coarse,
            rows_ref,
            (m_send.at[c, mine - 1], m_all.at[c, mine], m_send.at[c, mine + 1]),
        )

    def send_counts(c, source):
        for b in (source * 3, source * 3 + 2):

            @pl.when(exists(3 + b % 3))
            def _():
                send_m(c, b).start()

    def count_own(c, carry):
        count(c, 1, cand_ref)

        @pl.when(c == 0)
        def _():
            pl.semaphore_wait(barrier, near)
            for b in others:

                @pl.when(exists(b))
                def _():
                    send_t(b).start()

            for part in range(chunks):
                for side in range(2):

                    @pl.when(exists(7 if side else 1))
                    def _():
                        send_c(part, side).start()

        send_counts(c, 1)
        return carry

    lax.fori_loop(0, chunks, count_own, 0)

    gene_iota = (
        lax.broadcasted_iota(jnp.int32, (min(SPAN, gene_pad), LANES), 0)
        .astype(jnp.float32)
        .astype(jnp.bfloat16)
    )
    lane_iota = lax.broadcasted_iota(jnp.int32, (LANES, LANES), 1).astype(jnp.float32).astype(jnp.bfloat16)
    hot_one = jnp.ones((), jnp.bfloat16)
    hot_zero = jnp.zeros((), jnp.bfloat16)
    tok_all[4] = tok_ref[...]

    def fill_hot(k, carry):
        b = pick(EARLY, k)

        @pl.when(exists(b) & (b != 4))
        def _():
            recv_t(b).wait_recv()

        for c in range(chunks):
            ids = tok_all[b, 2:3, c * LANES : (c + 1) * LANES]
            for low in range(0, gene_pad, SPAN):
                high = min(low + SPAN, gene_pad)
                here = (ids - float(low)).astype(jnp.bfloat16)
                hot[low:high, at(b, c)] = jnp.where(gene_iota[: high - low] == here, hot_one, hot_zero)
        return carry

    lax.fori_loop(0, 9, fill_hot, 0)

    def fill_hot_rows(b, carry):
        for c in range(chunks):
            ids = tok_all[b, 2:3, c * LANES : (c + 1) * LANES]
            upright = jnp.broadcast_to(ids, (LANES, LANES)).T
            for low in range(0, gene_pad, LANES):
                here = (upright - float(low)).astype(jnp.bfloat16)
                hot_rows[at(b, c), low : low + LANES] = jnp.where(lane_iota == here, hot_one, hot_zero)
        return carry

    def count_lists(c, carry):
        for side, source in ((0, 0), (1, 2)):

            @pl.when(exists(source * 3 + 1))
            def _():
                recv_c(c, side).wait_recv()
                count(c, source, cand_all.at[side])
                send_counts(c, source)

        return carry

    lax.fori_loop(0, chunks, count_lists, 0)

    def hot_of(b):
        return hot[:, pl.ds(pl.multiple_of(b * tokens, LANES), tokens)]

    for it in range(ITERS):
        order = FIRST if it == 0 else LATE

        def look_up(k, gl):
            gl[...] = jnp.dot(table[...], hot_of(pick(order, k)), preferred_element_type=jnp.float32)

        def score_tile(k, gl, ahead):
            b = pick(order, k)
            dr, dc = offsets(b)
            if it == 0:

                @pl.when(exists(b) & (b % 3 != 1))
                def _():
                    for c in range(chunks):
                        recv_m(c, b).wait_recv()

            if ahead is not None:
                look_up(k + 1, ahead)
            each = [slice(c * LANES, (c + 1) * LANES) for c in range(chunks)]
            y0 = [tok_all[b, 0:1, lanes] + jnp.asarray(dr, jnp.float32) for lanes in each]
            y1 = [tok_all[b, 1:2, lanes] + jnp.asarray(dc, jnp.float32) for lanes in each]
            tops = [jnp.full((8, LANES), NEG, jnp.float32) for _ in each]
            for first in range(0, cells, 8):
                strip = slice(first, first + 8)
                mu0, mu1 = state[0, strip], state[1, strip]
                p00, p01, p11 = par[0, strip], par[1, strip], par[2, strip]
                for c, lanes in enumerate(each):
                    d0 = y0[c] - mu0
                    d1 = y1[c] - mu1
                    base = gl[strip, lanes]
                    for piece in range(1, PIECES):
                        base = base + gl[piece * cells + first : piece * cells + first + 8, lanes]
                    score = base - (d0 * (p00 * d0 + p01 * d1) + p11 * d1 * d1)
                    score = jnp.where(m_all[c, b, strip] > 0.0, score, NEG)
                    tops[c] = jnp.maximum(tops[c], score)
                    e_all[b, strip, lanes] = score
            tops = [jnp.max(top, axis=0, keepdims=True) for top in tops]
            sums = [jnp.zeros((8, LANES), jnp.float32) for _ in each]
            for first in range(0, cells, 8):
                strip = slice(first, first + 8)
                for c, lanes in enumerate(each):
                    terms = m_all[c, b, strip] * jnp.exp2(e_all[b, strip, lanes] - tops[c])
                    e_all[b, strip, lanes] = terms
                    sums[c] = sums[c] + terms
            for c, lanes in enumerate(each):
                stat_send[it, b, 0:1, lanes] = tops[c]
                stat_send[it, b, 1:2, lanes] = jnp.sum(sums[c], axis=0, keepdims=True)

            @pl.when(exists(b) & (b != 4))
            def _():
                send_s(it, b).start()

        look_up(0, gl_a)

        def score_pair(i, carry):
            score_tile(2 * i, gl_a, gl_b)
            score_tile(2 * i + 1, gl_b, gl_a)
            return carry

        lax.fori_loop(0, 4, score_pair, 0)
        score_tile(8, gl_a, None)

        if it == 0:
            lax.fori_loop(0, 9, fill_hot_rows, 0)
        stat_recv[it, 4] = stat_send[it, 4]
        for b in others:

            @pl.when(exists(b))
            def _():
                recv_s(it, b).wait_recv()

        top = stat_recv[it, 4, 0:1, :]
        for b in others:
            top = jnp.maximum(top, stat_recv[it, b, 0:1, :])
        total = jnp.zeros((1, tokens), jnp.float32)
        for b in range(9):
            total = total + stat_recv[it, b, 1:2, :] * jnp.exp2(stat_recv[it, b, 0:1, :] - top)
        scale = tok_ref[3:4, :] / total
        for b in (0, 2, 6, 8, 1, 7, 3, 5):
            fac_send[it, b] = scale * jnp.exp2(stat_recv[it, b, 0:1, :] - top)

            @pl.when(exists(b))
            def _():
                send_f(it, b).start()

        fac_recv[it, 4] = scale * jnp.exp2(stat_recv[it, 4, 0:1, :] - top)

        for j in range(6):
            acc[j] = jnp.zeros(wide, jnp.float32)
        counts[...] = jnp.zeros(counts.shape, jnp.float32)

        def count_genes(k, share):
            start = pl.multiple_of(pick(EARLY, k) * tokens, LANES)
            counts[...] += jnp.dot(share[...], hot_rows[pl.ds(start, tokens), :], preferred_element_type=jnp.float32)

        def sum_tile(k, share, behind):
            b = pick(EARLY, k)
            dr, dc = offsets(b)

            @pl.when(exists(b) & (b != 4))
            def _():
                recv_f(it, b).wait_recv()

            if behind is not None:
                count_genes(k - 1, behind)
            for first in range(0, cells, STRIP):
                strip = slice(first, first + STRIP)
                sums = None
                for c in range(chunks):
                    lanes = slice(c * LANES, (c + 1) * LANES)
                    y0 = tok_all[b, 0:1, lanes] + jnp.asarray(dr, jnp.float32)
                    y1 = tok_all[b, 1:2, lanes] + jnp.asarray(dc, jnp.float32)
                    post = e_all[b, strip, lanes] * fac_recv[it, b, :, lanes]
                    share[strip, lanes] = post.astype(jnp.bfloat16)
                    by0 = post * y0
                    by1 = post * y1
                    terms = (post, by0, by1, by0 * y0, by0 * y1, by1 * y1)
                    sums = terms if sums is None else tuple(x + y for x, y in zip(sums, terms))
                for j in range(6):
                    acc[j, strip, :] += sums[j]

        sum_tile(0, share_a, None)

        def sum_pair(i, carry):
            sum_tile(2 * i + 1, share_b, share_a)
            sum_tile(2 * i + 2, share_a, share_b)
            return carry

        lax.fori_loop(0, 4, sum_pair, 0)
        count_genes(8, share_a)

        mass, s0, s1, s00, s01, s11 = [
            jnp.broadcast_to(jnp.sum(acc[j], axis=1, keepdims=True), wide) for j in range(6)
        ]
        below = mass + prior_weight
        mu0 = (s0 + prior_weight * state[0]) / below
        mu1 = (s1 + prior_weight * state[1]) / below
        q00 = s00 - 2.0 * mu0 * s0 + mass * mu0 * mu0
        q01 = s01 - mu0 * s1 - mu1 * s0 + mass * mu0 * mu1
        q11 = s11 - 2.0 * mu1 * s1 + mass * mu1 * mu1
        state[0] = mu0
        state[1] = mu1
        state[2] = (q00 + prior_weight * state[2]) / below
        state[3] = (q01 + prior_weight * state[3]) / below
        state[4] = (q11 + prior_weight * state[4]) / below
        state[5] = jnp.log(mass + 1.0)
        if it + 1 < ITERS:
            fill_table(log_profile(counts[...], genes))

    fields = (
        state[0],
        state[1],
        0.5 * jnp.log(state[2]),
        0.5 * jnp.log(state[4]),
        state[3] / jnp.sqrt(state[2] * state[4]),
        state[5],
    )
    lane = lax.broadcasted_iota(jnp.int32, wide, 1)
    packed = jnp.zeros(wide, jnp.float32)
    for j, field in enumerate(fields):
        packed = jnp.where(lane == j, field, packed)
    cells_out[...] = packed.T[0:8, :]

    for b in others:

        @pl.when(exists(b))
        def _():
            send_t(b).wait_send()
            for it in range(ITERS):
                send_s(it, b).wait_send()
                send_f(it, b).wait_send()

    for source in range(3):
        for b in (source * 3, source * 3 + 2):

            @pl.when(exists(source * 3 + 1) & exists(b - source * 3 + 3))
            def _():
                for c in range(chunks):
                    send_m(c, b).wait_send()

    for side in range(2):

        @pl.when(exists(7 if side else 1))
        def _():
            for c in range(chunks):
                send_c(c, side).wait_send()


def run_em(rows, cols, live, cand, positions, gene_ids, weights, centroids, spreads, correlation):
    genes, cells = weights.shape
    tokens, slots = cand.shape
    chunks = tokens // LANES
    gene_pad = -(-genes // LANES) * LANES
    f32 = jnp.float32
    dma = pltpu.SemaphoreType.DMA
    return pl.pallas_call(
        functools.partial(em_kernel, rows, cols),
        in_specs=[pl.BlockSpec(memory_space=pltpu.SMEM)] + [pl.BlockSpec(memory_space=pltpu.VMEM)] * 7,
        out_specs=[pl.BlockSpec(memory_space=pltpu.VMEM)] * 2,
        out_shape=(
            jax.ShapeDtypeStruct((cells, gene_pad), f32),
            jax.ShapeDtypeStruct((8, cells), f32),
        ),
        scratch_shapes=[
            pltpu.VMEM((LANES * PITCH, cells), f32),
            pltpu.VMEM((2, tokens, slots), jnp.int32),
            pltpu.VMEM((chunks, 9, cells, LANES), f32),
            pltpu.VMEM((chunks, 9, cells, LANES), f32),
            pltpu.VMEM((8, tokens), f32),
            pltpu.VMEM((9, 8, tokens), f32),
            pltpu.VMEM((9, cells, tokens), f32),
            pltpu.VMEM((gene_pad, 9 * tokens), jnp.bfloat16),
            pltpu.VMEM((9 * tokens, gene_pad), jnp.bfloat16),
            pltpu.VMEM((PIECES * cells, gene_pad), jnp.bfloat16),
            pltpu.VMEM((PIECES * cells, tokens), f32),
            pltpu.VMEM((PIECES * cells, tokens), f32),
            pltpu.VMEM((3, cells, LANES), f32),
            pltpu.VMEM((6, cells, LANES), f32),
            pltpu.VMEM((6, cells, LANES), f32),
            pltpu.VMEM((cells, tokens), jnp.bfloat16),
            pltpu.VMEM((cells, tokens), jnp.bfloat16),
            pltpu.VMEM((ITERS, 9, 2, tokens), f32),
            pltpu.VMEM((ITERS, 9, 2, tokens), f32),
            pltpu.VMEM((ITERS, 9, 1, tokens), f32),
            pltpu.VMEM((ITERS, 9, 1, tokens), f32),
            dma((chunks, 2)),
            dma((chunks, 2)),
            dma((chunks, 9)),
            dma((chunks, 9)),
            dma((9,)),
            dma((9,)),
            dma((ITERS, 9)),
            dma((ITERS, 9)),
            dma((ITERS, 9)),
            dma((ITERS, 9)),
        ],
        compiler_params=pltpu.CompilerParams(collective_id=0, has_side_effects=True),
        name="em_cells",
    )(live, cand, positions, gene_ids, weights, centroids, spreads, correlation)


def finish_kernel(counts, summary, prof_out, cells_out):
    genes = prof_out.shape[0]
    prof_out[...] = log_profile(counts[...], genes).T[0:genes, :]
    for j in range(cells_out.shape[0]):
        cells_out[j, 0] = summary[j : j + 1, :]


def finish(genes, counts, summary):
    cells = counts.shape[0]
    return pl.pallas_call(
        finish_kernel,
        in_specs=[pl.BlockSpec(memory_space=pltpu.VMEM)] * 2,
        out_specs=[pl.BlockSpec(memory_space=pltpu.VMEM)] * 2,
        out_shape=(
            jax.ShapeDtypeStruct((genes, cells), jnp.float32),
            jax.ShapeDtypeStruct((6, 1, 1, cells), jnp.float32),
        ),
        name="finish",
    )(counts, summary)


def body(
    rows, cols, positions, genes, candidates, block_counts, profile_weights, centroids, spreads, correlation
):
    counts, summary = run_em(
        rows,
        cols,
        block_counts,
        candidates[0, 0],
        positions,
        genes,
        profile_weights[:, 0, 0, :],
        centroids,
        spreads,
        correlation,
    )
    profile, cell_rows = finish(profile_weights.shape[0], counts, summary)
    return (profile[:, None, None, :], cell_rows)


def solution(mesh):
    return jax.shard_map(
        functools.partial(body, mesh.shape["row"], mesh.shape["col"]),
        mesh=mesh,
        in_specs=(
            P(None, ("groups", "row"), "col", None),
            P(("groups", "row"), "col", None),
            P(("groups", "row"), "col", None, None),
            P(("groups", "row"), "col", None),
            P(None, ("groups", "row"), "col", None),
            P(None, ("groups", "row"), "col", None),
            P(None, ("groups", "row"), "col", None),
            P(("groups", "row"), "col", None),
        ),
        out_specs=(
            P(None, ("groups", "row"), "col", None),
            P(None, ("groups", "row"), "col", None),
        ),
        check_vma=False,
    )
```

```python
import functools

import jax
import jax.numpy as jnp
from jax import lax
from jax.experimental import pallas as pl
from jax.experimental.pallas import tpu as pltpu
from jax.sharding import PartitionSpec as P

ITERS = 2
LANES = 128
NEG = -3.0e38
PIECES = 2
SPAN = 256
STRIP = 32
FINE = 32
PITCH = 17
LOG2E = 1.4426950408889634
EARLY = (4, 3, 5, 1, 7, 0, 2, 6, 8)
LATE = (0, 2, 6, 8, 1, 7, 3, 5, 4)
FIRST = (1, 7, 4, 3, 5, 0, 2, 6, 8)

pseudo_count = 0.05
prior_weight = 1.0


def pick(order, k):
    if isinstance(k, int):
        return order[k]
    return sum(jnp.where(k == i, b, 0) for i, b in enumerate(order))


def log_profile(gene_counts, genes):
    total = jnp.sum(gene_counts, axis=1, keepdims=True) + genes * pseudo_count
    return jnp.log(gene_counts + pseudo_count) - jnp.log(total)


def count_chunk(cand_ref, first, low, rows_ref, outs):
    slots = cand_ref.shape[1]
    cells = outs[0].shape[0]
    coarse = cells // FINE
    bf16 = jnp.bfloat16
    fine_iota = lax.broadcasted_iota(jnp.int32, (FINE, slots), 0).astype(jnp.float32).astype(bf16)
    coarse_iota = lax.broadcasted_iota(jnp.int32, (16, slots), 0).astype(jnp.float32).astype(bf16)
    one = jnp.ones((), bf16)
    zero = jnp.zeros((), bf16)
    empty = jnp.zeros((16, slots), bf16)

    for start in range(0, LANES, 16):
        ids = cand_ref[pl.ds(pl.multiple_of(first + start, 16), 16), :]
        major = lax.div(ids, jnp.int32(FINE))
        minor = (ids - major * FINE).astype(jnp.float32).astype(bf16)
        major = (major - low).astype(jnp.float32).astype(bf16)
        for t in range(0, 16, 2):
            fine_hot = [jnp.where(fine_iota == minor[u : u + 1, :], one, zero) for u in (t, t + 1)]
            coarse_hot = [jnp.where(coarse_iota == major[u : u + 1, :], one, zero) for u in (t, t + 1)]
            left = jnp.concatenate(
                [
                    jnp.concatenate([coarse_hot[0], empty], axis=1),
                    jnp.concatenate([empty, coarse_hot[1]], axis=1),
                ],
                axis=0,
            )
            times = lax.dot_general(
                left,
                jnp.concatenate(fine_hot, axis=1),
                (((1,), (1,)), ((), ())),
                preferred_element_type=jnp.float32,
            )
            for u in (0, 1):
                row = (start + t + u) * PITCH
                rows_ref[row : row + 16, 0:FINE] = times[u * 16 : u * 16 + 16]

    for a in range(3):
        outs[a][...] = jnp.concatenate(
            [rows_ref[pl.ds(a * coarse + h, LANES, stride=PITCH), 0:FINE].T for h in range(coarse)], axis=0
        )


def em_kernel(
    rows, cols, live_ref, cand_ref, pos_ref, gene_ref, w_ref, cent_ref, spread_ref, corr_ref, counts, cells_out,
    rows_ref, cand_all, m_send, m_all, tok_ref, tok_all, e_all, hot, hot_rows, table, gl_a, gl_b, par, state, acc, share_a, share_b,
    stat_send, stat_recv, fac_send, fac_recv,
    cs_sem, cr_sem, ms_sem, mr_sem, ts_sem, tr_sem, ss_sem, sr_sem, fs_sem, fr_sem,
):
    genes, cells = w_ref.shape
    gene_pad = hot.shape[0]
    tokens = tok_ref.shape[1]
    chunks = tokens // LANES
    my_row = lax.axis_index("row")
    my_col = lax.axis_index("col")

    def offsets(b):
        return b // 3 - 1, b % 3 - 1

    def at(b, c):
        return pl.ds(pl.multiple_of(b * tokens + c * LANES, LANES), LANES)

    def exists(b):
        dr, dc = offsets(b)
        r, c = my_row + dr, my_col + dc
        return (r >= 0) & (r < rows) & (c >= 0) & (c < cols)

    def place(b):
        dr, dc = offsets(b)
        return {"row": my_row + dr, "col": my_col + dc}

    def remote(src, dst, send, recv, b):
        return pltpu.make_async_remote_copy(
            src_ref=src, dst_ref=dst, send_sem=send, recv_sem=recv,
            device_id=place(b), device_id_type=pl.DeviceIdType.MESH,
        )

    def send_c(c, side):
        part = pl.ds(pl.multiple_of(c * LANES, LANES), LANES)
        b = 7 if side else 1
        return remote(
            cand_ref.at[part], cand_all.at[1 - side, part], cs_sem.at[c, side], cr_sem.at[c, 1 - side], b
        )

    def recv_c(c, side):
        part = pl.ds(pl.multiple_of(c * LANES, LANES), LANES)
        b = 7 if side else 1
        return remote(
            cand_ref.at[part], cand_all.at[side, part], cs_sem.at[c, 1 - side], cr_sem.at[c, side], b
        )

    def across(b):
        return b + 2 - 2 * (b % 3)

    def column_place(b):
        return {"col": my_col + b % 3 - 1}

    def send_m(c, b):
        return pltpu.make_async_remote_copy(
            src_ref=m_send.at[c, b], dst_ref=m_all.at[c, across(b)],
            send_sem=ms_sem.at[c, b], recv_sem=mr_sem.at[c, across(b)],
            device_id=column_place(b), device_id_type=pl.DeviceIdType.MESH,
        )

    def recv_m(c, b):
        return pltpu.make_async_remote_copy(
            src_ref=m_send.at[c, across(b)], dst_ref=m_all.at[c, b],
            send_sem=ms_sem.at[c, across(b)], recv_sem=mr_sem.at[c, b],
            device_id=column_place(b), device_id_type=pl.DeviceIdType.MESH,
        )

    def send_t(b):
        return remote(tok_ref, tok_all.at[8 - b], ts_sem.at[b], tr_sem.at[8 - b], b)

    def recv_t(b):
        return remote(tok_ref, tok_all.at[b], ts_sem.at[8 - b], tr_sem.at[b], b)

    def send_s(it, b):
        return remote(stat_send.at[it, b], stat_recv.at[it, 8 - b], ss_sem.at[it, b], sr_sem.at[it, 8 - b], b)

    def recv_s(it, b):
        return remote(stat_send.at[it, 8 - b], stat_recv.at[it, b], ss_sem.at[it, 8 - b], sr_sem.at[it, b], b)

    def send_f(it, b):
        return remote(fac_send.at[it, b], fac_recv.at[it, 8 - b], fs_sem.at[it, b], fr_sem.at[it, 8 - b], b)

    def recv_f(it, b):
        return remote(fac_send.at[it, 8 - b], fac_recv.at[it, b], fs_sem.at[it, 8 - b], fr_sem.at[it, b], b)

    others = (1, 7, 0, 2, 6, 8, 3, 5)
    barrier = pltpu.get_barrier_semaphore()
    near = 0
    for b in others:
        near = near + exists(b).astype(jnp.int32)

        @pl.when(exists(b))
        def _():
            pl.semaphore_signal(barrier, inc=1, device_id=place(b), device_id_type=pl.DeviceIdType.MESH)

    tok_ref[0:1, :] = pos_ref[0, 0]
    tok_ref[1:2, :] = pos_ref[1, 0]
    tok_ref[2:3, :] = gene_ref[0].astype(jnp.float32)
    blocks = live_ref.shape[2]
    block = tokens // blocks
    for n in range(blocks):
        inside = lax.broadcasted_iota(jnp.int32, (1, block), 1) < live_ref[0, 0, n]
        tok_ref[3:4, n * block : (n + 1) * block] = jnp.where(inside, 1.0, 0.0)
    tok_ref[4:8, :] = jnp.zeros((4, tokens), jnp.float32)

    for b in others:

        @pl.when(jnp.logical_not(exists(b)))
        def _():
            tok_all[b] = jnp.zeros((8, tokens), jnp.float32)
            for c in range(chunks):
                m_all[c, b] = jnp.zeros((cells, LANES), jnp.float32)
            for it in range(ITERS):
                stat_recv[it, b, 0:1, :] = jnp.full((1, tokens), NEG, jnp.float32)
                stat_recv[it, b, 1:2, :] = jnp.zeros((1, tokens), jnp.float32)
                fac_recv[it, b] = jnp.zeros((1, tokens), jnp.float32)

    wide = (cells, LANES)
    acc[0] = jnp.zeros(wide, jnp.float32)
    acc[0, 0:1, :] = cent_ref[0, 0]
    acc[0, 1:2, :] = cent_ref[1, 0]
    acc[0, 2:3, :] = spread_ref[0, 0]
    acc[0, 3:4, :] = spread_ref[1, 0]
    acc[0, 4:5, :] = corr_ref[0]
    initial = acc[0].T

    def column(j):
        return jnp.broadcast_to(initial[:, j : j + 1], wide)

    sd_row, sd_col = column(2), column(3)
    state[0] = column(0)
    state[1] = column(1)
    state[2] = sd_row * sd_row
    state[3] = column(4) * sd_row * sd_col
    state[4] = sd_col * sd_col
    state[5] = jnp.zeros(wide, jnp.float32)

    def fill_table(logs):
        c00, c01, c11 = state[2], state[3], state[4]
        det = c00 * c11 - c01 * c01
        par[0] = (0.5 * LOG2E) * (c11 / det)
        par[1] = -LOG2E * (c01 / det)
        par[2] = (0.5 * LOG2E) * (c00 / det)
        bias = state[5] - 0.5 * jnp.log(det)
        for first in range(0, gene_pad, LANES):
            part = (logs[:, first : first + LANES] + bias) * LOG2E
            for piece in range(PIECES):
                rounded = part.astype(jnp.bfloat16)
                table[piece * cells : (piece + 1) * cells, first : first + LANES] = rounded
                part = part - rounded.astype(jnp.float32)

    weights = w_ref[...]
    logs = jnp.log(weights) - jnp.log(jnp.sum(weights, axis=0, keepdims=True))
    if gene_pad > genes:
        logs = jnp.concatenate([logs, jnp.zeros((gene_pad - genes, cells), jnp.float32)], axis=0)
    fill_table(logs.T)

    coarse = cells // FINE

    def count(c, source, list_ref):
        mine = source * 3 + 1
        count_chunk(
            list_ref,
            c * LANES,
            (2 - source) * 3 * coarse,
            rows_ref,
            (m_send.at[c, mine - 1], m_all.at[c, mine], m_send.at[c, mine + 1]),
        )

    def send_counts(c, source):
        for b in (source * 3, source * 3 + 2):

            @pl.when(exists(3 + b % 3))
            def _():
                send_m(c, b).start()

    def count_own(c, carry):
        count(c, 1, cand_ref)

        @pl.when(c == 0)
        def _():
            pl.semaphore_wait(barrier, near)
            for b in others:

                @pl.when(exists(b))
                def _():
                    send_t(b).start()

            for part in range(chunks):
                for side in range(2):

                    @pl.when(exists(7 if side else 1))
                    def _():
                        send_c(part, side).start()

        send_counts(c, 1)
        return carry

    lax.fori_loop(0, chunks, count_own, 0)

    gene_iota = (
        lax.broadcasted_iota(jnp.int32, (min(SPAN, gene_pad), LANES), 0)
        .astype(jnp.float32)
        .astype(jnp.bfloat16)
    )
    lane_iota = lax.broadcasted_iota(jnp.int32, (LANES, LANES), 1).astype(jnp.float32).astype(jnp.bfloat16)
    hot_one = jnp.ones((), jnp.bfloat16)
    hot_zero = jnp.zeros((), jnp.bfloat16)
    tok_all[4] = tok_ref[...]

    def fill_hot(k, carry):
        b = pick(EARLY, k)

        @pl.when(exists(b) & (b != 4))
        def _():
            recv_t(b).wait_recv()

        for c in range(chunks):
            ids = tok_all[b, 2:3, c * LANES : (c + 1) * LANES]
            for low in range(0, gene_pad, SPAN):
                high = min(low + SPAN, gene_pad)
                here = (ids - float(low)).astype(jnp.bfloat16)
                hot[low:high, at(b, c)] = jnp.where(gene_iota[: high - low] == here, hot_one, hot_zero)
        return carry

    lax.fori_loop(0, 9, fill_hot, 0)

    def fill_hot_rows(b, carry):
        for c in range(chunks):
            ids = tok_all[b, 2:3, c * LANES : (c + 1) * LANES]
            upright = jnp.broadcast_to(ids, (LANES, LANES)).T
            for low in range(0, gene_pad, LANES):
                here = (upright - float(low)).astype(jnp.bfloat16)
                hot_rows[at(b, c), low : low + LANES] = jnp.where(lane_iota == here, hot_one, hot_zero)
        return carry

    def count_lists(c, carry):
        for side, source in ((0, 0), (1, 2)):

            @pl.when(exists(source * 3 + 1))
            def _():
                recv_c(c, side).wait_recv()
                count(c, source, cand_all.at[side])
                send_counts(c, source)

        return carry

    lax.fori_loop(0, chunks, count_lists, 0)

    def hot_of(b):
        return hot[:, pl.ds(pl.multiple_of(b * tokens, LANES), tokens)]

    for it in range(ITERS):
        order = FIRST if it == 0 else LATE

        def look_up(k, gl):
            gl[...] = jnp.dot(table[...], hot_of(pick(order, k)), preferred_element_type=jnp.float32)

        def score_tile(k, gl, ahead):
            b = pick(order, k)
            dr, dc = offsets(b)
            if it == 0:

                @pl.when(exists(b) & (b % 3 != 1))
                def _():
                    for c in range(chunks):
                        recv_m(c, b).wait_recv()

            if ahead is not None:
                look_up(k + 1, ahead)
            each = [slice(c * LANES, (c + 1) * LANES) for c in range(chunks)]
            y0 = [tok_all[b, 0:1, lanes] + jnp.asarray(dr, jnp.float32) for lanes in each]
            y1 = [tok_all[b, 1:2, lanes] + jnp.asarray(dc, jnp.float32) for lanes in each]
            tops = [jnp.full((8, LANES), NEG, jnp.float32) for _ in each]
            for first in range(0, cells, 8):
                strip = slice(first, first + 8)
                mu0, mu1 = state[0, strip], state[1, strip]
                p00, p01, p11 = par[0, strip], par[1, strip], par[2, strip]
                for c, lanes in enumerate(each):
                    d0 = y0[c] - mu0
                    d1 = y1[c] - mu1
                    base = gl[strip, lanes]
                    for piece in range(1, PIECES):
                        base = base + gl[piece * cells + first : piece * cells + first + 8, lanes]
                    score = base - (d0 * (p00 * d0 + p01 * d1) + p11 * d1 * d1)
                    score = jnp.where(m_all[c, b, strip] > 0.0, score, NEG)
                    tops[c] = jnp.maximum(tops[c], score)
                    e_all[b, strip, lanes] = score
            tops = [jnp.max(top, axis=0, keepdims=True) for top in tops]
            sums = [jnp.zeros((8, LANES), jnp.float32) for _ in each]
            for first in range(0, cells, 8):
                strip = slice(first, first + 8)
                for c, lanes in enumerate(each):
                    terms = m_all[c, b, strip] * jnp.exp2(e_all[b, strip, lanes] - tops[c])
                    e_all[b, strip, lanes] = terms
                    sums[c] = sums[c] + terms
            for c, lanes in enumerate(each):
                stat_send[it, b, 0:1, lanes] = tops[c]
                stat_send[it, b, 1:2, lanes] = jnp.sum(sums[c], axis=0, keepdims=True)

            @pl.when(exists(b) & (b != 4))
            def _():
                send_s(it, b).start()

        look_up(0, gl_a)

        def score_pair(i, carry):
            score_tile(2 * i, gl_a, gl_b)
            score_tile(2 * i + 1, gl_b, gl_a)
            return carry

        lax.fori_loop(0, 4, score_pair, 0)
        score_tile(8, gl_a, None)

        if it == 0:
            lax.fori_loop(0, 9, fill_hot_rows, 0)
        stat_recv[it, 4] = stat_send[it, 4]
        for b in others:

            @pl.when(exists(b))
            def _():
                recv_s(it, b).wait_recv()

        top = stat_recv[it, 4, 0:1, :]
        for b in others:
            top = jnp.maximum(top, stat_recv[it, b, 0:1, :])
        total = jnp.zeros((1, tokens), jnp.float32)
        for b in range(9):
            total = total + stat_recv[it, b, 1:2, :] * jnp.exp2(stat_recv[it, b, 0:1, :] - top)
        scale = tok_ref[3:4, :] / total
        for b in (0, 2, 6, 8, 1, 7, 3, 5):
            fac_send[it, b] = scale * jnp.exp2(stat_recv[it, b, 0:1, :] - top)

            @pl.when(exists(b))
            def _():
                send_f(it, b).start()

        fac_recv[it, 4] = scale * jnp.exp2(stat_recv[it, 4, 0:1, :] - top)

        for j in range(6):
            acc[j] = jnp.zeros(wide, jnp.float32)
        counts[...] = jnp.zeros(counts.shape, jnp.float32)

        def count_genes(k, share):
            start = pl.multiple_of(pick(EARLY, k) * tokens, LANES)
            counts[...] += jnp.dot(share[...], hot_rows[pl.ds(start, tokens), :], preferred_element_type=jnp.float32)

        def sum_tile(k, share, behind):
            b = pick(EARLY, k)
            dr, dc = offsets(b)

            @pl.when(exists(b) & (b != 4))
            def _():
                recv_f(it, b).wait_recv()

            if behind is not None:
                count_genes(k - 1, behind)
            for first in range(0, cells, STRIP):
                strip = slice(first, first + STRIP)
                sums = None
                for c in range(chunks):
                    lanes = slice(c * LANES, (c + 1) * LANES)
                    y0 = tok_all[b, 0:1, lanes] + jnp.asarray(dr, jnp.float32)
                    y1 = tok_all[b, 1:2, lanes] + jnp.asarray(dc, jnp.float32)
                    post = e_all[b, strip, lanes] * fac_recv[it, b, :, lanes]
                    share[strip, lanes] = post.astype(jnp.bfloat16)
                    by0 = post * y0
                    by1 = post * y1
                    terms = (post, by0, by1, by0 * y0, by0 * y1, by1 * y1)
                    sums = terms if sums is None else tuple(x + y for x, y in zip(sums, terms))
                for j in range(6):
                    acc[j, strip, :] += sums[j]

        sum_tile(0, share_a, None)

        def sum_pair(i, carry):
            sum_tile(2 * i + 1, share_b, share_a)
            sum_tile(2 * i + 2, share_a, share_b)
            return carry

        lax.fori_loop(0, 4, sum_pair, 0)
        count_genes(8, share_a)

        mass, s0, s1, s00, s01, s11 = [
            jnp.broadcast_to(jnp.sum(acc[j], axis=1, keepdims=True), wide) for j in range(6)
        ]
        below = mass + prior_weight
        mu0 = (s0 + prior_weight * state[0]) / below
        mu1 = (s1 + prior_weight * state[1]) / below
        q00 = s00 - 2.0 * mu0 * s0 + mass * mu0 * mu0
        q01 = s01 - mu0 * s1 - mu1 * s0 + mass * mu0 * mu1
        q11 = s11 - 2.0 * mu1 * s1 + mass * mu1 * mu1
        state[0] = mu0
        state[1] = mu1
        state[2] = (q00 + prior_weight * state[2]) / below
        state[3] = (q01 + prior_weight * state[3]) / below
        state[4] = (q11 + prior_weight * state[4]) / below
        state[5] = jnp.log(mass + 1.0)
        if it + 1 < ITERS:
            fill_table(log_profile(counts[...], genes))

    fields = (
        state[0],
        state[1],
        0.5 * jnp.log(state[2]),
        0.5 * jnp.log(state[4]),
        state[3] / jnp.sqrt(state[2] * state[4]),
        state[5],
    )
    lane = lax.broadcasted_iota(jnp.int32, wide, 1)
    packed = jnp.zeros(wide, jnp.float32)
    for j, field in enumerate(fields):
        packed = jnp.where(lane == j, field, packed)
    cells_out[...] = packed.T[0:8, :]

    for b in others:

        @pl.when(exists(b))
        def _():
            send_t(b).wait_send()
            for it in range(ITERS):
                send_s(it, b).wait_send()
                send_f(it, b).wait_send()

    for source in range(3):
        for b in (source * 3, source * 3 + 2):

            @pl.when(exists(source * 3 + 1) & exists(b - source * 3 + 3))
            def _():
                for c in range(chunks):
                    send_m(c, b).wait_send()

    for side in range(2):

        @pl.when(exists(7 if side else 1))
        def _():
            for c in range(chunks):
                send_c(c, side).wait_send()


def run_em(rows, cols, live, cand, positions, gene_ids, weights, centroids, spreads, correlation):
    genes, cells = weights.shape
    tokens, slots = cand.shape
    chunks = tokens // LANES
    gene_pad = -(-genes // LANES) * LANES
    f32 = jnp.float32
    dma = pltpu.SemaphoreType.DMA
    return pl.pallas_call(
        functools.partial(em_kernel, rows, cols),
        in_specs=[pl.BlockSpec(memory_space=pltpu.SMEM)] + [pl.BlockSpec(memory_space=pltpu.VMEM)] * 7,
        out_specs=[pl.BlockSpec(memory_space=pltpu.VMEM)] * 2,
        out_shape=(
            jax.ShapeDtypeStruct((cells, gene_pad), f32),
            jax.ShapeDtypeStruct((8, cells), f32),
        ),
        scratch_shapes=[
            pltpu.VMEM((LANES * PITCH, cells), f32),
            pltpu.VMEM((2, tokens, slots), jnp.int32),
            pltpu.VMEM((chunks, 9, cells, LANES), f32),
            pltpu.VMEM((chunks, 9, cells, LANES), f32),
            pltpu.VMEM((8, tokens), f32),
            pltpu.VMEM((9, 8, tokens), f32),
            pltpu.VMEM((9, cells, tokens), f32),
            pltpu.VMEM((gene_pad, 9 * tokens), jnp.bfloat16),
            pltpu.VMEM((9 * tokens, gene_pad), jnp.bfloat16),
            pltpu.VMEM((PIECES * cells, gene_pad), jnp.bfloat16),
            pltpu.VMEM((PIECES * cells, tokens), f32),
            pltpu.VMEM((PIECES * cells, tokens), f32),
            pltpu.VMEM((3, cells, LANES), f32),
            pltpu.VMEM((6, cells, LANES), f32),
            pltpu.VMEM((6, cells, LANES), f32),
            pltpu.VMEM((cells, tokens), jnp.bfloat16),
            pltpu.VMEM((cells, tokens), jnp.bfloat16),
            pltpu.VMEM((ITERS, 9, 2, tokens), f32),
            pltpu.VMEM((ITERS, 9, 2, tokens), f32),
            pltpu.VMEM((ITERS, 9, 1, tokens), f32),
            pltpu.VMEM((ITERS, 9, 1, tokens), f32),
            dma((chunks, 2)),
            dma((chunks, 2)),
            dma((chunks, 9)),
            dma((chunks, 9)),
            dma((9,)),
            dma((9,)),
            dma((ITERS, 9)),
            dma((ITERS, 9)),
            dma((ITERS, 9)),
            dma((ITERS, 9)),
        ],
        compiler_params=pltpu.CompilerParams(collective_id=0, has_side_effects=True),
        name="em_cells",
    )(live, cand, positions, gene_ids, weights, centroids, spreads, correlation)


def finish_kernel(counts, summary, prof_out, cells_out):
    genes = prof_out.shape[0]
    prof_out[...] = log_profile(counts[...], genes).T[0:genes, :]
    for j in range(cells_out.shape[0]):
        cells_out[j, 0] = summary[j : j + 1, :]


def finish(genes, counts, summary):
    cells = counts.shape[0]
    return pl.pallas_call(
        finish_kernel,
        in_specs=[pl.BlockSpec(memory_space=pltpu.VMEM)] * 2,
        out_specs=[pl.BlockSpec(memory_space=pltpu.VMEM)] * 2,
        out_shape=(
            jax.ShapeDtypeStruct((genes, cells), jnp.float32),
            jax.ShapeDtypeStruct((6, 1, 1, cells), jnp.float32),
        ),
        name="finish",
    )(counts, summary)


def body(
    rows, cols, positions, genes, candidates, block_counts, profile_weights, centroids, spreads, correlation
):
    counts, summary = run_em(
        rows,
        cols,
        block_counts,
        candidates[0, 0],
        positions,
        genes,
        profile_weights[:, 0, 0, :],
        centroids,
        spreads,
        correlation,
    )
    profile, cell_rows = finish(profile_weights.shape[0], counts, summary)
    return (profile[:, None, None, :], cell_rows)


def solution(mesh):
    return jax.shard_map(
        functools.partial(body, mesh.shape["row"], mesh.shape["col"]),
        mesh=mesh,
        in_specs=(
            P(None, ("groups", "row"), "col", None),
            P(("groups", "row"), "col", None),
            P(("groups", "row"), "col", None, None),
            P(("groups", "row"), "col", None),
            P(None, ("groups", "row"), "col", None),
            P(None, ("groups", "row"), "col", None),
            P(None, ("groups", "row"), "col", None),
            P(("groups", "row"), "col", None),
        ),
        out_specs=(
            P(None, ("groups", "row"), "col", None),
            P(None, ("groups", "row"), "col", None),
        ),
        check_vma=False,
    )
```
